32 devices in a mesh: cfg: 2 (over x), space: 16 (over z, y, core).
Axes of the slice: x: 2, y: 2, z: 4, core: 2. Of those that a mesh axis runs over, the one named last changes fastest.
Arguments:
- vectors: float32 [4, 2, 3, 2048, 256], P('cfg', None, None, 'space'), parts along dimension 0, may hold values from -1.75 to 1.75
- links: float32 [4, 3, 2, 3, 3, 2048], P('cfg', None, None, None, None, 'space'), parts along dimension 0, may hold values from -2.5 to 2.5
- directions: int32 [3], replicated, may hold values from 0 to 2
- slice_group: int32 [2], replicated, may hold values from 0 to 1, as said below
- peram: float32 [4, 1024, 1024], P('cfg', None, 'space'), parts along dimension 0, may hold values from -0.3125 to 0.3125
- block_group: int32 [16], P('space'), may hold values from 0 to 1
Outputs:
- elementals: float32 [4, 3, 2, 256, 256], P('cfg', None, None, 'space'), parts along dimension 0
- blocks: float32 [4, 1024, 64], P('cfg', 'space'), parts along dimension 0
The draws below stay inside these ranges and needn't reach their ends.
There are 2 independent parts, one for each index of `cfg`. The reference program is written for one: setup_inputs(seed, part) draws one part's arguments, and reference() takes and returns one part's arrays. A program takes and returns all parts, laid end to end along the dimension named above; an argument that names none is the same for every part. Nothing has to cross between parts.
Inputs may be any that keep to these rules, and one draw needn't show every extreme that they name: `slice_group`: every group holds at least one timeslice.
All inputs are finite; a program needn't handle non-finite values.
Results may differ from the reference program's by a relative error of at most 0.0001.
Values sent between devices are 32-bit elements; how exact they have to be, the bound alone decides.
No kernel may reach another device: no remote copies, remote signals or barrier semaphores. Data moves between devices by JAX's collectives and lax.ppermute only.
A program may use at most 64 MiB of HBM per device.

```python
import jax
import jax.numpy as jnp
import numpy as np
from jax import lax

NV = 256
NT = 2
NG = 2
LY = 16
LZ = 16
LX = 8
SITES = 2048
CB = 64
N_SPACE = 16


def draw_slice_group(key, part):
    group_key, order_key = jax.random.split(jax.random.fold_in(key, 11))
    base = jax.random.randint(group_key, (NT,), 0, NG, dtype=jnp.int32)
    order = jax.random.permutation(order_key, jnp.arange(NT, dtype=jnp.int32))
    return base.at[order[:NG]].set(jnp.arange(NG, dtype=jnp.int32))


def with_ends(entries, rng, smallest, largest):
    longest = entries.shape.index(max(entries.shape))
    spots = []
    for shift in (0, 1):
        where = [jax.random.randint(jax.random.fold_in(rng, axis), (), 0, length) for axis, length in enumerate(entries.shape)]
        where[longest] = (where[longest] + shift) % entries.shape[longest]
        spots.append(tuple(where))
    return entries.at[spots[0]].set(smallest).at[spots[1]].set(largest)


def shard_levels(own_key, shape, pieces, least, top_value):
    loudness, own = 1.0, jax.random.fold_in(own_key, 6)
    for dim, parts in pieces:
        steps = jnp.exp(jax.random.uniform(jax.random.fold_in(own, dim), (parts,), jnp.float32, least / len(pieces), top_value / len(pieces)))
        loudness = loudness * jnp.repeat(steps, shape[dim] // parts).reshape([-1 if axis == dim else 1 for axis in range(len(shape))])
    return loudness


def scatter_about(rng, shape, scale, limit, cuts=(), held_as=jnp.bfloat16):
    factor_of = shard_levels(rng, shape, cuts, -0.22, 0.18) if cuts else 1.0
    result = jax.random.normal(rng, shape, jnp.float32) * scale * factor_of
    return jnp.minimum(jnp.maximum(result, -limit), limit).astype(held_as)


def setup_inputs(seed: int = 0, part: int = 0) -> dict:
    key_list = jax.random.split(jax.random.key(seed), 7)
    own_keys = jax.random.split(jax.random.fold_in(key_list[6], part), 7)
    vectors = scatter_about(own_keys[0], (NT, 2, 3, SITES, NV), ((3 * SITES) ** -0.25), 1.75, ((3, 16),), jnp.float32)
    links = scatter_about(own_keys[1], (NT, 3, 2, 3, 3, SITES), 6 ** -0.5, 2.5, ((5, 16),), jnp.float32)
    directions = jax.random.randint(key_list[2], (3,), 0, 3).astype(jnp.int32)
    slice_group = draw_slice_group(jax.random.fold_in(key_list[6], 71), part)
    peram = scatter_about(own_keys[4], (2, 4 * NV, 4 * NV), ((8 * NV) ** -0.5), 0.3125, ((2, 16),), jnp.float32)
    block_group = with_ends(jax.random.randint(key_list[5], (N_SPACE,), 0, NG), jax.random.fold_in(key_list[5], 1), 0, NG - 1).astype(jnp.int32)
    return dict(vectors=vectors, links=links, directions=directions, slice_group=slice_group, peram=peram, block_group=block_group)


precise = lax.Precision.HIGHEST


def gamma_tables():
    pauli_one = np.array([[0.0, 1.0], [1.0, 0.0]])
    pauli_three = np.array([[1.0, 0.0], [0.0, -1.0]])
    rotate = np.array([[0.0, -1.0], [1.0, 0.0]])
    real_part = np.zeros((3, 4, 4))
    imag_part = np.zeros((3, 4, 4))
    imag_part[0, :2, 2:] = -pauli_one
    imag_part[0, 2:, :2] = pauli_one
    real_part[1, :2, 2:] = rotate
    real_part[1, 2:, :2] = -rotate
    imag_part[2, :2, 2:] = -pauli_three
    imag_part[2, 2:, :2] = pauli_three
    return jnp.asarray(real_part, jnp.float32), jnp.asarray(imag_part, jnp.float32)


def apply_link(matrix, vector_field):
    link_real = matrix[0][..., None]
    link_imag = matrix[1][..., None]
    vec_real = vector_field[0][None]
    vec_imag = vector_field[1][None]
    real_part = jnp.sum(link_real * vec_real - link_imag * vec_imag, axis=1)
    imag_part = jnp.sum(link_real * vec_imag + link_imag * vec_real, axis=1)
    return jnp.stack([real_part, imag_part])


def apply_adjoint(matrix, vector_field):
    link_real = jnp.swapaxes(matrix[0], 0, 1)[..., None]
    link_imag = jnp.swapaxes(matrix[1], 0, 1)[..., None]
    vec_real = vector_field[0][None]
    vec_imag = vector_field[1][None]
    real_part = jnp.sum(link_real * vec_real + link_imag * vec_imag, axis=1)
    imag_part = jnp.sum(link_real * vec_imag - link_imag * vec_real, axis=1)
    return jnp.stack([real_part, imag_part])


def contract(vector_field, derived):
    width = vector_field.shape[-1]
    left_rows = vector_field.reshape(-1, width)
    right_real = derived.reshape(-1, width)
    right_imag = jnp.stack([derived[1], -derived[0]]).reshape(-1, width)
    real_part = jnp.einsum("kv,kw->vw", left_rows, right_real, precision=precise)
    imag_part = jnp.einsum("kv,kw->vw", left_rows, right_imag, precision=precise)
    return jnp.stack([real_part, imag_part])


def reference(vectors, links, directions, slice_group, peram, block_group):
    field_all = vectors.reshape(NT, 2, 3, LX, LY, LZ, NV)
    gauge_all = links.reshape(NT, 3, 2, 3, 3, LX, LY, LZ)
    per_time = []
    for tslice in range(NT):
        eigen_field = field_all[tslice]
        elem_terms = []
        for axis_index in range(3):
            matrix = gauge_all[tslice, axis_index]
            ahead_field = jnp.roll(eigen_field, -1, axis=2 + axis_index)
            behind = jnp.roll(apply_adjoint(matrix, eigen_field), 1, axis=2 + axis_index)
            derived = 0.5 * (apply_link(matrix, ahead_field) - behind)
            elem_terms.append(contract(eigen_field, derived))
        per_time.append(jnp.stack(elem_terms))
    by_direction = jnp.stack(per_time)
    direction_hot = (directions[:, None] == jnp.arange(3, dtype=jnp.int32)[None, :]).astype(jnp.float32)
    chosen = jnp.einsum("ki,tirvw->tkrvw", direction_hot, by_direction, precision=precise)
    group_hot = (slice_group[:, None] == jnp.arange(NG, dtype=jnp.int32)[None, :]).astype(jnp.float32)
    elementals = jnp.einsum("tg,tkrvw->gkrvw", group_hot, chosen, precision=precise)
    gamma_real, gamma_imag = gamma_tables()
    col_blocks = peram.reshape(2, 4, NV, N_SPACE, CB)
    peram_real = col_blocks[0]
    peram_imag = col_blocks[1]
    block_hot = (block_group[:, None] == jnp.arange(NG, dtype=jnp.int32)[None, :]).astype(jnp.float32)
    picked = jnp.einsum("jg,gkrvw->jkrvw", block_hot, elementals, precision=precise)
    elem_real = picked[:, :, 0]
    elem_imag = picked[:, :, 1]
    mid_real = (jnp.einsum("jkvw,swjc->jksvc", elem_real, peram_real, precision=precise)
                - jnp.einsum("jkvw,swjc->jksvc", elem_imag, peram_imag, precision=precise))
    mid_imag = (jnp.einsum("jkvw,swjc->jksvc", elem_real, peram_imag, precision=precise)
                + jnp.einsum("jkvw,swjc->jksvc", elem_imag, peram_real, precision=precise))
    out_real = (jnp.einsum("kab,jkbvc->javc", gamma_real, mid_real, precision=precise)
                - jnp.einsum("kab,jkbvc->javc", gamma_imag, mid_imag, precision=precise))
    out_imag = (jnp.einsum("kab,jkbvc->javc", gamma_real, mid_imag, precision=precise)
                + jnp.einsum("kab,jkbvc->javc", gamma_imag, mid_real, precision=precise))
    res_real = (jnp.einsum("avjc,javd->jcd", peram_real, out_real, precision=precise)
                + jnp.einsum("avjc,javd->jcd", peram_imag, out_imag, precision=precise))
    res_imag = (jnp.einsum("avjc,javd->jcd", peram_real, out_imag, precision=precise)
                - jnp.einsum("avjc,javd->jcd", peram_imag, out_real, precision=precise))
    blocks = jnp.stack([res_real, res_imag]).reshape(2, N_SPACE * CB, CB)
    return elementals, blocks
```

```python
import functools

import jax
import jax.numpy as jnp
from jax import lax
from jax.experimental import pallas as pl
from jax.experimental.pallas import tpu as pltpu
from jax.sharding import PartitionSpec as P

LZ = 16
VMEM = pl.BlockSpec(memory_space=pltpu.VMEM)
SMEM = pl.BlockSpec(memory_space=pltpu.SMEM)
NT_DIMS = (((1,), (1,)), ((), ()))
NN_DIMS = (((1,), (0,)), ((), ()))


def split(value):
    high = value.astype(jnp.bfloat16)
    low = (value - high.astype(jnp.float32)).astype(jnp.bfloat16)
    return high, low


def dot3(left, right, dims):
    dot = functools.partial(
        lax.dot_general, dimension_numbers=dims, preferred_element_type=jnp.float32
    )
    return dot(left[0], right[0]) + dot(left[0], right[1]) + dot(left[1], right[0])


def store_left(v_ref, left_ref):
    sites, width = v_ref.shape[2], v_ref.shape[3]
    for part in range(2):
        for colour in range(3):
            high, low = split(v_ref[part, colour].T)
            at = (part * 3 + colour) * sites
            other = ((1 - part) * 3 + colour) * sites
            for level, value in enumerate((high, low)):
                left_ref[level, :width, at : at + sites] = value
                left_ref[level, width:, other : other + sites] = value if part else -value


def store_right(right_ref, row, sites, sources):
    alpha = [None] * 3
    beta = [None] * 3

    def add(total, term):
        return term if total is None else total + term

    for coef, base, field in sources:
        for b in range(3):
            plus = field[0][b] + field[1][b]
            minus = field[0][b] - field[1][b]
            for a in range(3):
                at = base + a * 3 + b
                real = coef[:, at : at + 1]
                imag = coef[:, at + 9 : at + 10]
                alpha[a] = add(add(alpha[a], real * plus), imag * minus)
                beta[a] = add(add(beta[a], imag * plus), -(real * minus))
    for part, values in enumerate((alpha, beta)):
        for a in range(3):
            high, low = split(values[a])
            at = (part * 3 + a) * sites + row * LZ
            right_ref[0, at : at + LZ, :] = high
            right_ref[1, at : at + LZ, :] = low


def load_row(v_ref, row):
    return [[v_ref[p, c, row * LZ : (row + 1) * LZ, :] for c in range(3)] for p in range(2)]


def contract(left_ref, right_ref):
    left = (left_ref[0], left_ref[1])
    right = (right_ref[0], right_ref[1])
    both = dot3(left, right, NN_DIMS)
    width = right_ref.shape[2]
    return both[:width] - both[width:].T


def plane_yz(v_ref, halo_ref, coef_ref, left_ref, right_ref):
    sites = v_ref.shape[2]
    rows = sites // LZ
    for row in range(rows):
        coef = coef_ref[row * LZ : (row + 1) * LZ, :]
        field = load_row(v_ref, row + 1) if row + 1 < rows else load_row(halo_ref, 0)
        store_right(right_ref, row, sites, [(coef, 0, field)])
    yield contract(left_ref, right_ref)
    for row in range(rows):
        coef = coef_ref[row * LZ : (row + 1) * LZ, :]
        field = [[pltpu.roll(x, LZ - 1, 0) for x in part] for part in load_row(v_ref, row)]
        store_right(right_ref, row, sites, [(coef, 18, field)])
    yield contract(left_ref, right_ref)


def own_kernel(v_ref, halo_ref, coef_ref, out_ref, left_ref, right_ref):
    store_left(v_ref, left_ref)
    for i, value in enumerate(plane_yz(v_ref, halo_ref, coef_ref, left_ref, right_ref)):
        out_ref[i] = value


def main_kernel(place_ref, va_ref, vb_ref, vc_ref, halo_ref, coef_ref, own_ref,
                keep_ref, send_ref, left_ref, right_ref, total_ref):
    sites, width = vb_ref.shape[2], vb_ref.shape[3]
    store_left(vb_ref, left_ref)
    for i, value in enumerate(plane_yz(vb_ref, halo_ref, coef_ref, left_ref, right_ref)):
        total_ref[(i + 1) * width : (i + 2) * width, :] = value + own_ref[i]
    for row in range(sites // LZ):
        coef = coef_ref[row * LZ : (row + 1) * LZ, :]
        sources = [(coef, 36, load_row(va_ref, row)), (coef, 54, load_row(vc_ref, row))]
        store_right(right_ref, row, sites, sources)
    total_ref[:width, :] = contract(left_ref, right_ref)
    core = place_ref[0] % 2
    half = 3 * width // 2
    keep_ref[...] = total_ref[pl.ds(pl.multiple_of(core * half, 8), half), :]
    send_ref[...] = total_ref[pl.ds(pl.multiple_of((1 - core) * half, 8), half), :]


def spread_kernel(place_ref, keep_ref, got_ref, *refs):
    outs, total_ref = refs[:-1], refs[-1]
    total_ref[...] = keep_ref[...] + got_ref[...]
    count = len(outs)
    size = outs[0].shape[0]
    pair = place_ref[0] // 4
    for d in range(count):
        at = lax.rem(pair + d, count) * size
        outs[d][...] = total_ref[pl.ds(pl.multiple_of(at, 8), size), :]


def sum_kernel(*refs):
    total = refs[0][...]
    for ref in refs[1:-1]:
        total = total + ref[...]
    refs[-1][...] = total


def table_kernel(p_ref, b_high, b_low, q_high, q_low):
    width = p_ref.shape[2] // 4
    cols = p_ref.shape[1]

    def spin(part, a):
        return p_ref[part, :, a * width : (a + 1) * width]

    m = [0.5 * (spin(0, a) - spin(1, a)) for a in (2, 3)]
    s = [0.5 * (spin(0, a) + spin(1, a)) for a in (2, 3)]
    pieces = {"m0": split(m[0]), "m1": split(m[1]), "s0": split(s[0]), "s1": split(s[1])}
    table = (
        ("+m1", "+s1", "+m0", "+s0"),
        ("+s1", "-m1", "-s0", "+m0"),
        ("+m0", "+s0", "-m1", "-s1"),
        ("-s1", "+m1", "-s0", "+m0"),
        ("+m1", "+s1", "-m0", "-s0"),
        ("-s0", "+m0", "+s1", "-m1"),
    )
    for k, names in enumerate(table):
        for j, name in enumerate(names):
            high, low = pieces[name[1:]]
            if name[0] == "-":
                high, low = -high, -low
            where = (slice(j * cols, (j + 1) * cols), slice(k * width, (k + 1) * width))
            b_high[where] = high
            b_low[where] = low
    for a in range(2):
        for part in range(2):
            high, low = split(spin(part, a))
            at = (a * 2 + part) * width
            q_high[:, at : at + width] = high
            q_low[:, at : at + width] = low


def take(ref, at, rows):
    if rows % 8 == 0:
        return ref[pl.ds(pl.multiple_of(at, 8), rows), :]
    inner = lax.rem(at, 8)
    tile = ref[pl.ds(pl.multiple_of(at - inner, 8), 8), :]
    return pltpu.roll(tile, lax.rem(8 - inner, 8), 0)[:rows]


def final_kernel(place_ref, direct_ref, slice_ref, block_ref, b_high, b_low, q_high, q_low,
                 *refs):
    count = (len(refs) - 4) // 4
    pieces = refs[: 4 * count]
    elem_ref, out_ref, all_ref, turn_ref = refs[4 * count :]
    size, width = pieces[0].shape
    place = place_ref[0]
    core = place % 2
    odd = (place // 2) % 2
    pair = place // 4
    half = 3 * width // 2
    for side in range(2):
        for other in range(2):
            for d in range(count):
                time = (odd + other) % 2
                base = (time * 2 + (core + side) % 2) * half
                at = base + lax.rem(pair - d + count, count) * size
                piece = pieces[(side * 2 + other) * count + d]
                all_ref[pl.ds(pl.multiple_of(at, 8), size), :] = piece[...]
    rows = elem_ref.shape[3]
    first = place * rows
    lane = pl.multiple_of((first // 128) * 128, 128)
    for i in range(6):
        block = all_ref[i * width : (i + 1) * width, pl.ds(lane, 128)]
        turn_ref[i * 128 : (i + 1) * 128, :] = block.T
    inner = lax.rem(first, 128)
    for g in range(2):
        time = jnp.where(slice_ref[0] == g, 0, 1)
        for k in range(3):
            which = time * 3 + direct_ref[k]
            row = take(all_ref, which * width + first, rows)
            col = take(turn_ref, which * 128 + inner, rows)
            elem_ref[g, k, 0] = 0.5 * (row - col)
            elem_ref[g, k, 1] = 0.5 * (row + col)
    time = jnp.where(slice_ref[0] == block_ref[0], 0, 1)
    turned = None
    for k in range(3):
        at = pl.multiple_of((time * 3 + direct_ref[k]) * width, 8)
        parts = split(all_ref[pl.ds(at, width), :])
        one = slice(k * width, (k + 1) * width)
        two = slice((3 + k) * width, (4 + k) * width)
        term = dot3((b_high[:, one], b_low[:, one]), parts, NT_DIMS) + dot3(
            (b_high[:, two], b_low[:, two]), parts, NN_DIMS
        )
        turned = term if turned is None else turned + term
    cols = q_high.shape[0]
    y = [turned[j * cols : (j + 1) * cols] for j in range(4)]
    same = split(jnp.concatenate([y[0], y[1], y[2], y[3]], axis=1))
    cross = split(jnp.concatenate([y[1], -y[0], y[3], -y[2]], axis=1))
    q = (q_high[...], q_low[...])
    out_ref[0] = dot3(q, cross, NT_DIMS) - dot3(cross, q, NT_DIMS)
    out_ref[1] = -(dot3(q, same, NT_DIMS) + dot3(same, q, NT_DIMS))


def shape(*dims, dtype=jnp.float32):
    return jax.ShapeDtypeStruct(dims, dtype)


def call(kernel, out, operands, scalars=0, scratch=(), flops=0):
    outs = jax.tree.leaves(out)
    moved = sum(x.size * x.dtype.itemsize for x in list(operands) + outs)
    return pl.pallas_call(
        kernel,
        out_shape=out,
        in_specs=[SMEM] * scalars + [VMEM] * (len(operands) - scalars),
        out_specs=jax.tree.map(lambda _: VMEM, out),
        scratch_shapes=list(scratch),
        cost_estimate=pl.CostEstimate(flops=flops, bytes_accessed=moved, transcendentals=0),
        name=kernel.__name__,
    )(*operands)


def body(vectors, links, directions, slice_group, peram, block_group):
    total = lax.axis_size("space")
    place = lax.axis_index("space")
    places = jnp.full((1,), place, jnp.int32)
    sites, width = vectors.shape[3], vectors.shape[4]
    pairs = total // 4
    odd = (place // 2) % 2

    def send(value, where):
        route = []
        for i in range(total):
            pair, o, core = where(i // 4, (i // 2) % 2, i % 2)
            route.append((i, ((pair % pairs) * 2 + o) * 2 + core))
        return lax.ppermute(value, "space", route)

    partner = lambda pair, o, core: (pair, 1 - o, core)
    across = lambda pair, o, core: (pair, 1 - o, 1 - core)
    twin = lambda pair, o, core: (pair, o, 1 - core)
    along = lambda pair, o, core: (pair + (1 if o else -1), o, core)

    def shift(d):
        return lambda pair, o, core: (pair + d, o, core)

    mine = lax.dynamic_index_in_dim(vectors, odd, 0, keepdims=False)
    theirs = lax.dynamic_index_in_dim(vectors, 1 - odd, 0, keepdims=False)
    flat = (0.5 * links).reshape(links.shape[0], 54, sites)
    link_a = lax.dynamic_index_in_dim(flat, odd, 0, keepdims=False)
    link_b = send(lax.dynamic_index_in_dim(flat, 1 - odd, 0, keepdims=False), partner)
    link_c = send(link_a[:18], along)
    halo_a = send(mine[:, :, :LZ], twin)
    halo_b = send(theirs[:, :, :LZ], across)
    vec_b = send(theirs, partner)
    vec_c = send(mine, along)

    def adjoint(matrix):
        matrix = matrix.reshape(2, 3, 3, sites)
        turned = jnp.swapaxes(matrix, 1, 2)
        return jnp.stack([-turned[0], turned[1]]).reshape(18, sites)

    one = jnp.where(odd == 0, adjoint(link_a[:18]), link_b[:18])
    two = jnp.where(odd == 0, link_b[:18], adjoint(link_c))
    coef_a = link_a[18:].T
    coef_b = jnp.concatenate([link_b[18:], one, two]).T

    left = pltpu.VMEM((2, 2 * width, 6 * sites), jnp.bfloat16)
    right = pltpu.VMEM((2, 6 * sites, width), jnp.bfloat16)
    work = 6 * 6 * sites * 2 * width * width
    own = call(own_kernel, shape(2, width, width), (mine, halo_a, coef_a),
               scratch=(left, right), flops=2 * work)
    half = 3 * width // 2
    keep, give = call(
        main_kernel, (shape(half, width),) * 2,
        (places, mine, vec_b, vec_c, halo_b, coef_b, own), scalars=1,
        scratch=(left, right, pltpu.VMEM((3 * width, width), jnp.float32)), flops=3 * work)
    got = send(give, twin)
    size = half // pairs
    spread = call(spread_kernel, (shape(size, width),) * pairs, (places, keep, got), scalars=1,
                  scratch=(pltpu.VMEM((half, width), jnp.float32),))
    parts = [spread[0]] + [send(spread[d], shift(d)) for d in range(1, pairs)]
    shard = call(sum_kernel, shape(size, width), parts)
    here = [shard] + [send(shard, shift(d)) for d in range(1, pairs)]
    there = [send(x, partner) for x in here]
    pieces = here + there
    pieces = pieces + [send(x, twin) for x in pieces]

    cols = peram.shape[2]
    turned = jnp.swapaxes(peram, 1, 2)
    bf16 = jnp.bfloat16
    tables = call(
        table_kernel,
        (shape(4 * cols, 6 * width, dtype=bf16),) * 2 + (shape(cols, 4 * width, dtype=bf16),) * 2,
        (turned,))
    return call(
        final_kernel,
        (shape(2, 3, 2, width // total, width), shape(2, cols, cols)),
        (places, directions, slice_group, block_group, *tables, *pieces), scalars=4,
        scratch=(pltpu.VMEM((6 * width, width), jnp.float32),
                 pltpu.VMEM((6 * 128, width), jnp.float32)),
        flops=36 * cols * width * width)


def solution(mesh):
    return jax.shard_map(
        body,
        mesh=mesh,
        in_specs=(
            P("cfg", None, None, "space", None),
            P("cfg", None, None, None, None, "space"),
            P(),
            P(),
            P("cfg", None, "space"),
            P("space"),
        ),
        out_specs=(P("cfg", None, None, "space", None), P("cfg", "space", None)),
        check_vma=False,
    )
```

```python
import functools

import jax
import jax.numpy as jnp
import numpy as np
from jax import lax
from jax.experimental import pallas as pl
from jax.experimental.pallas import tpu as pltpu
from jax.sharding import PartitionSpec as P

LZ = 16
VMEM = pl.BlockSpec(memory_space=pltpu.VMEM)
SMEM = pl.BlockSpec(memory_space=pltpu.SMEM)
NT_DIMS = (((1,), (1,)), ((), ()))
NN_DIMS = (((1,), (0,)), ((), ()))


def split(value):
    high = value.astype(jnp.bfloat16)
    low = (value - high.astype(jnp.float32)).astype(jnp.bfloat16)
    return high, low


def dot3(left, right, dims):
    dot = functools.partial(
        lax.dot_general, dimension_numbers=dims, preferred_element_type=jnp.float32
    )
    return dot(left[0], right[0]) + dot(left[0], right[1]) + dot(left[1], right[0])


def store_left(v_ref, left_ref):
    sites, width = v_ref.shape[2], v_ref.shape[3]
    for part in range(2):
        for colour in range(3):
            high, low = split(v_ref[part, colour].T)
            at = (part * 3 + colour) * sites
            other = ((1 - part) * 3 + colour) * sites
            for level, value in enumerate((high, low)):
                left_ref[level, :width, at : at + sites] = value
                left_ref[level, width:, other : other + sites] = value if part else -value


def add(total, term):
    return term if total is None else total + term


def store_right(right_ref, row, sites, sources):
    width = right_ref.shape[2]
    coefs = []
    for coef, base, _ in sources:
        wide = [jnp.broadcast_to(coef[:, base + j : base + j + 1], (LZ, 128)) for j in range(18)]
        coefs.append(wide)
    for lanes in range(0, width, 128):
        cut = slice(lanes, lanes + 128)
        fields = []
        for _, _, field in sources:
            real, imag = field(cut)
            fields.append(([r + i for r, i in zip(real, imag)], [r - i for r, i in zip(real, imag)]))
        for a in range(3):
            alpha = beta = None
            for wide, (plus, minus) in zip(coefs, fields):
                for b in range(3):
                    real, imag = wide[a * 6 + b * 2], wide[a * 6 + b * 2 + 1]
                    alpha = add(add(alpha, real * plus[b]), imag * minus[b])
                    beta = add(add(beta, imag * plus[b]), -(real * minus[b]))
            for part, value in enumerate((alpha, beta)):
                high, low = split(value)
                at = (part * 3 + a) * sites + row * LZ
                right_ref[0, at : at + LZ, cut] = high
                right_ref[1, at : at + LZ, cut] = low


def row_of(v_ref, row, turn=False):
    def load(cut):
        at = slice(row * LZ, (row + 1) * LZ)
        parts = [[v_ref[p, c, at, cut] for c in range(3)] for p in range(2)]
        if turn:
            parts = [[pltpu.roll(x, LZ - 1, 0) for x in part] for part in parts]
        return parts

    return load


def adjoint_rows(rows):
    out = []
    for a in range(3):
        for b in range(3):
            at = b * 6 + a * 2
            out += [-rows[at : at + 1], rows[at + 1 : at + 2]]
    return jnp.concatenate(out, axis=0)


def of_time(ref, odd):
    count = ref.shape[0] // 2
    return 0.5 * jnp.where(odd == 0, ref[:count], ref[count:])


def contract(left_ref, right_ref):
    left = (left_ref[0], left_ref[1])
    right = (right_ref[0], right_ref[1])
    both = dot3(left, right, NN_DIMS)
    width = right_ref.shape[2]
    return both[:width] - both[width:].T


def plane_yz(v_ref, halo_ref, coef, left_ref, right_ref):
    sites = v_ref.shape[2]
    rows = sites // LZ
    for row in range(rows):
        here = coef[row * LZ : (row + 1) * LZ]
        ahead = row_of(v_ref, row + 1) if row + 1 < rows else row_of(halo_ref, 0)
        store_right(right_ref.at[0], row, sites, [(here, 18, ahead)])
        store_right(right_ref.at[1], row, sites, [(here, 36, row_of(v_ref, row, turn=True))])
    return [contract(left_ref, right_ref.at[i]) for i in range(2)]


def own_kernel(place_ref, v_ref, halo_ref, link_ref, out_ref, left_ref, right_ref, coef_ref):
    odd = (place_ref[0] // 2) % 2
    coef_ref[:54, :] = of_time(link_ref, odd)
    store_left(v_ref, left_ref)
    coef = coef_ref[...].T
    for i, value in enumerate(plane_yz(v_ref, halo_ref, coef, left_ref, right_ref)):
        out_ref[i] = value


def main_kernel(place_ref, va_ref, vb_ref, vc_ref, halo_ref, link_a, link_b, link_c, own_ref,
                keep_ref, send_ref, left_ref, right_ref, coef_ref, total_ref):
    sites, width = vb_ref.shape[2], vb_ref.shape[3]
    odd = (place_ref[0] // 2) % 2
    coef_ref[:54, :] = of_time(link_b, odd)
    there = coef_ref[:18, :]
    before = adjoint_rows(of_time(link_a, odd)[:18])
    after = adjoint_rows(of_time(link_c, odd)[:18])
    coef_ref[56:74, :] = jnp.where(odd == 0, before, there)
    coef_ref[80:98, :] = jnp.where(odd == 0, there, after)
    coef = coef_ref[...].T
    store_left(vb_ref, left_ref)
    for i, value in enumerate(plane_yz(vb_ref, halo_ref, coef, left_ref, right_ref)):
        total_ref[(i + 1) * width : (i + 2) * width, :] = value + own_ref[i]
    for row in range(sites // LZ):
        here = coef[row * LZ : (row + 1) * LZ]
        sources = [(here, 56, row_of(va_ref, row)), (here, 80, row_of(vc_ref, row))]
        store_right(right_ref.at[2], row, sites, sources)
    total_ref[:width, :] = contract(left_ref, right_ref.at[2])
    core = place_ref[0] % 2
    half = 3 * width // 2
    keep_ref[...] = total_ref[pl.ds(pl.multiple_of(core * half, 8), half), :]
    send_ref[...] = total_ref[pl.ds(pl.multiple_of((1 - core) * half, 8), half), :]


def spread_kernel(place_ref, keep_ref, got_ref, *refs):
    outs, total_ref = refs[:-1], refs[-1]
    total_ref[...] = keep_ref[...] + got_ref[...]
    count = len(outs)
    size = outs[0].shape[0]
    pair = place_ref[0] // 4
    for d in range(count):
        at = lax.rem(pair + d, count) * size
        outs[d][...] = total_ref[pl.ds(pl.multiple_of(at, 8), size), :]


def sum_kernel(*refs):
    total = refs[0][...]
    for ref in refs[1:-1]:
        total = total + ref[...]
    refs[-1][...] = total


def table_kernel(p_ref, b_high, b_low, q_high, q_low):
    width = p_ref.shape[2] // 4
    cols = p_ref.shape[1]

    def spin(part, a):
        return p_ref[part, :, a * width : (a + 1) * width]

    m = [0.5 * (spin(0, a) - spin(1, a)) for a in (2, 3)]
    s = [0.5 * (spin(0, a) + spin(1, a)) for a in (2, 3)]
    pieces = {"m0": split(m[0]), "m1": split(m[1]), "s0": split(s[0]), "s1": split(s[1])}
    table = (
        ("+m1", "+s1", "+m0", "+s0"),
        ("+s1", "-m1", "-s0", "+m0"),
        ("+m0", "+s0", "-m1", "-s1"),
        ("-s1", "+m1", "-s0", "+m0"),
        ("+m1", "+s1", "-m0", "-s0"),
        ("-s0", "+m0", "+s1", "-m1"),
    )
    for k, names in enumerate(table):
        for j, name in enumerate(names):
            high, low = pieces[name[1:]]
            if name[0] == "-":
                high, low = -high, -low
            where = (slice(j * cols, (j + 1) * cols), slice(k * width, (k + 1) * width))
            b_high[where] = high
            b_low[where] = low
    for a in range(2):
        for part in range(2):
            high, low = split(spin(part, a))
            at = (a * 2 + part) * width
            q_high[:, at : at + width] = high
            q_low[:, at : at + width] = low


def take(ref, at, rows):
    if rows % 8 == 0:
        return ref[pl.ds(pl.multiple_of(at, 8), rows), :]
    inner = lax.rem(at, 8)
    tile = ref[pl.ds(pl.multiple_of(at - inner, 8), 8), :]
    return pltpu.roll(tile, lax.rem(8 - inner, 8), 0)[:rows]


def final_kernel(place_ref, direct_ref, slice_ref, block_ref, b_high, b_low, q_high, q_low,
                 *refs):
    count = (len(refs) - 4) // 4
    pieces = refs[: 4 * count]
    elem_ref, out_ref, all_ref, turn_ref = refs[4 * count :]
    size, width = pieces[0].shape
    place = place_ref[0]
    core = place % 2
    odd = (place // 2) % 2
    pair = place // 4
    half = 3 * width // 2
    for side in range(2):
        for other in range(2):
            for d in range(count):
                time = (odd + other) % 2
                base = (time * 2 + (core + side) % 2) * half
                at = base + lax.rem(pair - d + count, count) * size
                piece = pieces[(side * 2 + other) * count + d]
                all_ref[pl.ds(pl.multiple_of(at, 8), size), :] = piece[...]
    rows = elem_ref.shape[3]
    first = place * rows
    lane = pl.multiple_of((first // 128) * 128, 128)
    for i in range(6):
        block = all_ref[i * width : (i + 1) * width, pl.ds(lane, 128)]
        turn_ref[i * 128 : (i + 1) * 128, :] = block.T
    inner = lax.rem(first, 128)
    for g in range(2):
        time = jnp.where(slice_ref[0] == g, 0, 1)
        for k in range(3):
            which = time * 3 + direct_ref[k]
            row = take(all_ref, which * width + first, rows)
            col = take(turn_ref, which * 128 + inner, rows)
            elem_ref[g, k, 0] = 0.5 * (row - col)
            elem_ref[g, k, 1] = 0.5 * (row + col)
    time = jnp.where(slice_ref[0] == block_ref[0], 0, 1)
    turned = None
    for k in range(3):
        at = pl.multiple_of((time * 3 + direct_ref[k]) * width, 8)
        parts = split(all_ref[pl.ds(at, width), :])
        one = slice(k * width, (k + 1) * width)
        two = slice((3 + k) * width, (4 + k) * width)
        term = dot3((b_high[:, one], b_low[:, one]), parts, NT_DIMS) + dot3(
            (b_high[:, two], b_low[:, two]), parts, NN_DIMS
        )
        turned = term if turned is None else turned + term
    cols = q_high.shape[0]
    y = [turned[j * cols : (j + 1) * cols] for j in range(4)]
    same = split(jnp.concatenate([y[0], y[1], y[2], y[3]], axis=1))
    cross = split(jnp.concatenate([y[1], -y[0], y[3], -y[2]], axis=1))
    q = (q_high[...], q_low[...])
    out_ref[0] = dot3(q, cross, NT_DIMS) - dot3(cross, q, NT_DIMS)
    out_ref[1] = -(dot3(q, same, NT_DIMS) + dot3(same, q, NT_DIMS))


def shape(*dims, dtype=jnp.float32):
    return jax.ShapeDtypeStruct(dims, dtype)


def size_of(x):
    return x.size * jnp.dtype(x.dtype).itemsize


def call(kernel, out, operands, scalars=0, scratch=(), flops=0):
    outs = jax.tree.leaves(out)
    moved = sum(size_of(x) for x in list(operands) + outs)
    held = sum(int(np.prod(x.shape)) * jnp.dtype(x.dtype).itemsize for x in scratch)
    limit = moved + held + (4 << 20)
    return pl.pallas_call(
        kernel,
        out_shape=out,
        in_specs=[SMEM] * scalars + [VMEM] * (len(operands) - scalars),
        out_specs=jax.tree.map(lambda _: VMEM, out),
        scratch_shapes=list(scratch),
        cost_estimate=pl.CostEstimate(flops=flops, bytes_accessed=moved, transcendentals=0),
        compiler_params=pltpu.CompilerParams(vmem_limit_bytes=limit),
    )(*operands)


def program(vectors, links, directions, slice_group, peram, block_group):
    total = lax.axis_size("space")
    place = lax.axis_index("space")
    places = jnp.full((1,), place, jnp.int32)
    sites, width = vectors.shape[3], vectors.shape[4]
    pairs = total // 4
    odd = (place // 2) % 2

    def send(value, where):
        route = []
        for i in range(total):
            pair, o, core = where(i // 4, (i // 2) % 2, i % 2)
            route.append((i, ((pair % pairs) * 2 + o) * 2 + core))
        return lax.ppermute(value, "space", route)

    partner = lambda pair, o, core: (pair, 1 - o, core)
    across = lambda pair, o, core: (pair, 1 - o, 1 - core)
    twin = lambda pair, o, core: (pair, o, 1 - core)
    along = lambda pair, o, core: (pair + (1 if o else -1), o, core)

    def shift(d):
        return lambda pair, o, core: (pair + d, o, core)

    flat = links.transpose(0, 1, 3, 4, 2, 5).reshape(links.shape[0] * 54, sites)
    link_b = send(flat, partner)
    link_c = send(flat, along)
    theirs = lax.dynamic_index_in_dim(vectors, 1 - odd, 0, keepdims=False)
    mine = lax.dynamic_index_in_dim(vectors, odd, 0, keepdims=False)
    vec_b = send(theirs, partner)
    vec_c = send(mine, along)
    halo_a = send(mine[:, :, :LZ], twin)
    halo_b = send(theirs[:, :, :LZ], across)

    left = pltpu.VMEM((2, 2 * width, 6 * sites), jnp.bfloat16)
    right = lambda n: pltpu.VMEM((n, 2, 6 * sites, width), jnp.bfloat16)
    coef = pltpu.VMEM((128, sites), jnp.float32)
    work = 6 * 6 * sites * 2 * width * width
    own = call(own_kernel, shape(2, width, width), (places, mine, halo_a, flat), scalars=1,
               scratch=(left, right(2), coef), flops=2 * work)
    cols = peram.shape[2]
    turned = jnp.swapaxes(peram, 1, 2)
    bf16 = jnp.bfloat16
    tables = call(
        table_kernel,
        (shape(4 * cols, 6 * width, dtype=bf16),) * 2
        + (shape(cols, 4 * width, dtype=bf16),) * 2,
        (turned,))
    half = 3 * width // 2
    keep, give = call(
        main_kernel, (shape(half, width),) * 2,
        (places, mine, vec_b, vec_c, halo_b, flat, link_b, link_c, own), scalars=1,
        scratch=(left, right(3), coef, pltpu.VMEM((3 * width, width), jnp.float32)),
        flops=3 * work)
    got = send(give, twin)
    size = half // pairs
    spread = call(spread_kernel, (shape(size, width),) * pairs, (places, keep, got), scalars=1,
                  scratch=(pltpu.VMEM((half, width), jnp.float32),))
    parts = [spread[0]] + [send(spread[d], shift(d)) for d in range(1, pairs)]
    shard = call(sum_kernel, shape(size, width), parts)
    here = [shard] + [send(shard, shift(d)) for d in range(1, pairs)]
    there = [send(x, partner) for x in here]
    pieces = here + there
    pieces = pieces + [send(x, twin) for x in pieces]

    return call(
        final_kernel,
        (shape(2, 3, 2, width // total, width), shape(2, cols, cols)),
        (places, directions, slice_group, block_group, *tables, *pieces), scalars=4,
        scratch=(pltpu.VMEM((6 * width, width), jnp.float32),
                 pltpu.VMEM((6 * 128, width), jnp.float32)),
        flops=36 * cols * width * width)


def solution(mesh):
    return jax.shard_map(
        program,
        mesh=mesh,
        in_specs=(
            P("cfg", None, None, "space", None),
            P("cfg", None, None, None, None, "space"),
            P(),
            P(),
            P("cfg", None, "space"),
            P("space"),
        ),
        out_specs=(P("cfg", None, None, "space", None), P("cfg", "space", None)),
        check_vma=False,
    )
```

```python
import functools

import jax
import jax.numpy as jnp
import numpy as np
from jax import lax
from jax.experimental import pallas as pl
from jax.experimental.pallas import tpu as pltpu
from jax.sharding import PartitionSpec as P

LZ = 16
VMEM = pl.BlockSpec(memory_space=pltpu.VMEM)
SMEM = pl.BlockSpec(memory_space=pltpu.SMEM)
NT_DIMS = (((1,), (1,)), ((), ()))
NN_DIMS = (((1,), (0,)), ((), ()))


def split(value):
    high = value.astype(jnp.bfloat16)
    low = (value - high.astype(jnp.float32)).astype(jnp.bfloat16)
    return high, low


def dot3(left, right, dims):
    dot = functools.partial(
        lax.dot_general, dimension_numbers=dims, preferred_element_type=jnp.float32
    )
    return dot(left[0], right[0]) + dot(left[0], right[1]) + dot(left[1], right[0])


def store_left(v_ref, left_ref):
    sites, width = v_ref.shape[2], v_ref.shape[3]
    for part in range(2):
        for colour in range(3):
            high, low = split(v_ref[part, colour].T)
            at = (part * 3 + colour) * sites
            other = ((1 - part) * 3 + colour) * sites
            for level, value in enumerate((high, low)):
                left_ref[level, :width, at : at + sites] = value
                left_ref[level, width:, other : other + sites] = value if part else -value


def add(total, term):
    return term if total is None else total + term


def store_right(right_ref, row, sites, sources):
    width = right_ref.shape[2]
    coefs = []
    for coef, base, _ in sources:
        wide = [jnp.broadcast_to(coef[:, base + j : base + j + 1], (LZ, 128)) for j in range(18)]
        coefs.append(wide)
    for lanes in range(0, width, 128):
        cut = slice(lanes, lanes + 128)
        fields = []
        for _, _, field in sources:
            real, imag = field(cut)
            fields.append(([r + i for r, i in zip(real, imag)], [r - i for r, i in zip(real, imag)]))
        for a in range(3):
            alpha = beta = None
            for wide, (plus, minus) in zip(coefs, fields):
                for b in range(3):
                    real, imag = wide[a * 6 + b * 2], wide[a * 6 + b * 2 + 1]
                    alpha = add(add(alpha, real * plus[b]), imag * minus[b])
                    beta = add(add(beta, imag * plus[b]), -(real * minus[b]))
            for part, value in enumerate((alpha, beta)):
                high, low = split(value)
                at = (part * 3 + a) * sites + row * LZ
                right_ref[0, at : at + LZ, cut] = high
                right_ref[1, at : at + LZ, cut] = low


def row_of(v_ref, row, turn=False):
    def load(cut):
        at = slice(row * LZ, (row + 1) * LZ)
        parts = [[v_ref[p, c, at, cut] for c in range(3)] for p in range(2)]
        if turn:
            parts = [[pltpu.roll(x, LZ - 1, 0) for x in part] for part in parts]
        return parts

    return load


def adjoint_rows(rows):
    out = []
    for a in range(3):
        for b in range(3):
            at = b * 6 + a * 2
            out += [-rows[at : at + 1], rows[at + 1 : at + 2]]
    return jnp.concatenate(out, axis=0)


def of_time(ref, odd):
    count = ref.shape[0] // 2
    return 0.5 * jnp.where(odd == 0, ref[:count], ref[count:])


def contract(left_ref, right_ref):
    left = (left_ref[0], left_ref[1])
    right = (right_ref[0], right_ref[1])
    both = dot3(left, right, NN_DIMS)
    width = right_ref.shape[2]
    return both[:width] - both[width:].T


def plane_yz(v_ref, halo_ref, coef, left_ref, right_ref):
    sites = v_ref.shape[2]
    rows = sites // LZ
    for row in range(rows):
        here = coef[row * LZ : (row + 1) * LZ]
        ahead = row_of(v_ref, row + 1) if row + 1 < rows else row_of(halo_ref, 0)
        store_right(right_ref.at[0], row, sites, [(here, 18, ahead)])
        store_right(right_ref.at[1], row, sites, [(here, 36, row_of(v_ref, row, turn=True))])
    return [contract(left_ref, right_ref.at[i]) for i in range(2)]


def own_kernel(place_ref, v_ref, halo_ref, link_ref, out_ref, left_ref, right_ref, coef_ref):
    odd = (place_ref[0] // 2) % 2
    coef_ref[:54, :] = of_time(link_ref, odd)
    store_left(v_ref, left_ref)
    coef = coef_ref[...].T
    for i, value in enumerate(plane_yz(v_ref, halo_ref, coef, left_ref, right_ref)):
        out_ref[i] = value


def main_kernel(place_ref, va_ref, vb_ref, vc_ref, halo_ref, link_a, link_b, link_c, own_ref,
                keep_ref, send_ref, left_ref, right_ref, coef_ref, total_ref):
    sites, width = vb_ref.shape[2], vb_ref.shape[3]
    odd = (place_ref[0] // 2) % 2
    coef_ref[:54, :] = of_time(link_b, odd)
    there = coef_ref[:18, :]
    before = adjoint_rows(of_time(link_a, odd)[:18])
    after = adjoint_rows(of_time(link_c, odd)[:18])
    coef_ref[56:74, :] = jnp.where(odd == 0, before, there)
    coef_ref[80:98, :] = jnp.where(odd == 0, there, after)
    coef = coef_ref[...].T
    store_left(vb_ref, left_ref)
    for i, value in enumerate(plane_yz(vb_ref, halo_ref, coef, left_ref, right_ref)):
        total_ref[(i + 1) * width : (i + 2) * width, :] = value + own_ref[i]
    for row in range(sites // LZ):
        here = coef[row * LZ : (row + 1) * LZ]
        sources = [(here, 56, row_of(va_ref, row)), (here, 80, row_of(vc_ref, row))]
        store_right(right_ref.at[2], row, sites, sources)
    total_ref[:width, :] = contract(left_ref, right_ref.at[2])
    core = place_ref[0] % 2
    half = 3 * width // 2
    keep_ref[...] = total_ref[pl.ds(pl.multiple_of(core * half, 8), half), :]
    send_ref[...] = total_ref[pl.ds(pl.multiple_of((1 - core) * half, 8), half), :]


def spread_kernel(place_ref, keep_ref, got_ref, *refs):
    outs, total_ref = refs[:-1], refs[-1]
    total_ref[...] = keep_ref[...] + got_ref[...]
    count = len(outs)
    size = outs[0].shape[0]
    pair = place_ref[0] // 4
    for d in range(count):
        at = (pair ^ d) * size
        outs[d][...] = total_ref[pl.ds(pl.multiple_of(at, 8), size), :]


def sum_kernel(*refs):
    total = refs[0][...]
    for ref in refs[1:-1]:
        total = total + ref[...]
    refs[-1][...] = total


def table_kernel(p_ref, b_high, b_low, q_high, q_low):
    width = p_ref.shape[2] // 4
    cols = p_ref.shape[1]

    def spin(part, a):
        return p_ref[part, :, a * width : (a + 1) * width]

    m = [0.5 * (spin(0, a) - spin(1, a)) for a in (2, 3)]
    s = [0.5 * (spin(0, a) + spin(1, a)) for a in (2, 3)]
    pieces = {"m0": split(m[0]), "m1": split(m[1]), "s0": split(s[0]), "s1": split(s[1])}
    table = (
        ("+m1", "+s1", "+m0", "+s0"),
        ("+s1", "-m1", "-s0", "+m0"),
        ("+m0", "+s0", "-m1", "-s1"),
        ("-s1", "+m1", "-s0", "+m0"),
        ("+m1", "+s1", "-m0", "-s0"),
        ("-s0", "+m0", "+s1", "-m1"),
    )
    for k, names in enumerate(table):
        for j, name in enumerate(names):
            high, low = pieces[name[1:]]
            if name[0] == "-":
                high, low = -high, -low
            where = (slice(j * cols, (j + 1) * cols), slice(k * width, (k + 1) * width))
            b_high[where] = high
            b_low[where] = low
    for a in range(2):
        for part in range(2):
            high, low = split(spin(part, a))
            at = (a * 2 + part) * width
            q_high[:, at : at + width] = high
            q_low[:, at : at + width] = low


def take(ref, at, rows):
    if rows % 8 == 0:
        return ref[pl.ds(pl.multiple_of(at, 8), rows), :]
    inner = lax.rem(at, 8)
    tile = ref[pl.ds(pl.multiple_of(at - inner, 8), 8), :]
    return pltpu.roll(tile, lax.rem(8 - inner, 8), 0)[:rows]


def final_kernel(place_ref, direct_ref, slice_ref, block_ref, b_high, b_low, q_high, q_low,
                 *refs):
    count = (len(refs) - 4) // 4
    pieces = refs[: 4 * count]
    elem_ref, out_ref, all_ref, turn_ref = refs[4 * count :]
    size, width = pieces[0].shape
    place = place_ref[0]
    core = place % 2
    odd = (place // 2) % 2
    pair = place // 4
    half = 3 * width // 2
    for side in range(2):
        for other in range(2):
            for d in range(count):
                time = (odd + other) % 2
                base = (time * 2 + (core + side) % 2) * half
                at = base + (pair ^ d) * size
                piece = pieces[(side * 2 + other) * count + d]
                all_ref[pl.ds(pl.multiple_of(at, 8), size), :] = piece[...]
    rows = elem_ref.shape[3]
    first = place * rows
    lane = pl.multiple_of((first // 128) * 128, 128)
    for i in range(6):
        block = all_ref[i * width : (i + 1) * width, pl.ds(lane, 128)]
        turn_ref[i * 128 : (i + 1) * 128, :] = block.T
    inner = lax.rem(first, 128)
    for g in range(2):
        time = jnp.where(slice_ref[0] == g, 0, 1)
        for k in range(3):
            which = time * 3 + direct_ref[k]
            row = take(all_ref, which * width + first, rows)
            col = take(turn_ref, which * 128 + inner, rows)
            elem_ref[g, k, 0] = 0.5 * (row - col)
            elem_ref[g, k, 1] = 0.5 * (row + col)
    time = jnp.where(slice_ref[0] == block_ref[0], 0, 1)
    turned = None
    for k in range(3):
        at = pl.multiple_of((time * 3 + direct_ref[k]) * width, 8)
        parts = split(all_ref[pl.ds(at, width), :])
        one = slice(k * width, (k + 1) * width)
        two = slice((3 + k) * width, (4 + k) * width)
        term = dot3((b_high[:, one], b_low[:, one]), parts, NT_DIMS) + dot3(
            (b_high[:, two], b_low[:, two]), parts, NN_DIMS
        )
        turned = term if turned is None else turned + term
    cols = q_high.shape[0]
    y = [turned[j * cols : (j + 1) * cols] for j in range(4)]
    same = split(jnp.concatenate([y[0], y[1], y[2], y[3]], axis=1))
    cross = split(jnp.concatenate([y[1], -y[0], y[3], -y[2]], axis=1))
    q = (q_high[...], q_low[...])
    out_ref[0] = dot3(q, cross, NT_DIMS) - dot3(cross, q, NT_DIMS)
    out_ref[1] = -(dot3(q, same, NT_DIMS) + dot3(same, q, NT_DIMS))


def shape(*dims, dtype=jnp.float32):
    return jax.ShapeDtypeStruct(dims, dtype)


def size_of(x):
    return x.size * jnp.dtype(x.dtype).itemsize


def call(kernel, out, operands, scalars=0, scratch=(), flops=0):
    outs = jax.tree.leaves(out)
    moved = sum(size_of(x) for x in list(operands) + outs)
    held = sum(int(np.prod(x.shape)) * jnp.dtype(x.dtype).itemsize for x in scratch)
    limit = moved + held + (4 << 20)
    return pl.pallas_call(
        kernel,
        out_shape=out,
        in_specs=[SMEM] * scalars + [VMEM] * (len(operands) - scalars),
        out_specs=jax.tree.map(lambda _: VMEM, out),
        scratch_shapes=list(scratch),
        cost_estimate=pl.CostEstimate(flops=flops, bytes_accessed=moved, transcendentals=0),
        compiler_params=pltpu.CompilerParams(vmem_limit_bytes=limit),
    )(*operands)


def program(vectors, links, directions, slice_group, peram, block_group):
    total = lax.axis_size("space")
    place = lax.axis_index("space")
    places = jnp.full((1,), place, jnp.int32)
    sites, width = vectors.shape[3], vectors.shape[4]
    pairs = total // 4
    odd = (place // 2) % 2

    def send(value, where):
        route = []
        for i in range(total):
            pair, o, core = where(i // 4, (i // 2) % 2, i % 2)
            route.append((i, ((pair % pairs) * 2 + o) * 2 + core))
        return lax.ppermute(value, "space", route)

    partner = lambda pair, o, core: (pair, 1 - o, core)
    across = lambda pair, o, core: (pair, 1 - o, 1 - core)
    twin = lambda pair, o, core: (pair, o, 1 - core)
    along = lambda pair, o, core: (pair + (1 if o else -1), o, core)

    def hop(d):
        return lambda pair, o, core: (pair ^ d, o, core)

    hops = sorted(range(1, pairs), key=lambda d: (d & 1, -d))
    if pairs == 4:
        hops = [2, 1, 3]

    flat = links.transpose(0, 1, 3, 4, 2, 5).reshape(links.shape[0] * 54, sites)
    theirs = lax.dynamic_index_in_dim(vectors, 1 - odd, 0, keepdims=False)
    vectors, theirs = lax.optimization_barrier((vectors, theirs))
    vec_b = send(theirs, partner)
    mine = lax.dynamic_index_in_dim(vectors, odd, 0, keepdims=False)
    vec_c = send(mine, along)
    link_b = send(flat, partner)
    link_c = send(flat, along)
    halo_a = send(mine[:, :, :LZ], twin)
    halo_b = send(theirs[:, :, :LZ], across)

    left = pltpu.VMEM((2, 2 * width, 6 * sites), jnp.bfloat16)
    right = lambda n: pltpu.VMEM((n, 2, 6 * sites, width), jnp.bfloat16)
    coef = pltpu.VMEM((128, sites), jnp.float32)
    work = 6 * 6 * sites * 2 * width * width
    own = call(own_kernel, shape(2, width, width), (places, mine, halo_a, flat), scalars=1,
               scratch=(left, right(2), coef), flops=2 * work)
    cols = peram.shape[2]
    turned = jnp.swapaxes(peram, 1, 2)
    bf16 = jnp.bfloat16
    tables = call(
        table_kernel,
        (shape(4 * cols, 6 * width, dtype=bf16),) * 2
        + (shape(cols, 4 * width, dtype=bf16),) * 2,
        (turned,))
    half = 3 * width // 2
    keep, give = call(
        main_kernel, (shape(half, width),) * 2,
        (places, mine, vec_b, vec_c, halo_b, flat, link_b, link_c, own), scalars=1,
        scratch=(left, right(3), coef, pltpu.VMEM((3 * width, width), jnp.float32)),
        flops=3 * work)
    got = send(give, twin)
    size = half // pairs
    spread = call(spread_kernel, (shape(size, width),) * pairs, (places, keep, got), scalars=1,
                  scratch=(pltpu.VMEM((half, width), jnp.float32),))
    parts = [spread[0]]
    for d in hops:
        parts.append(send(spread[d], hop(d)))
    shard = call(sum_kernel, shape(size, width), parts)
    here = {0: shard}
    for d in hops:
        here[d] = send(shard, hop(d))
    there = {}
    for d in [0] + hops:
        there[d] = send(here[d], partner)
    pieces = [here[d] for d in range(pairs)] + [there[d] for d in range(pairs)]
    pieces = pieces + [send(x, twin) for x in pieces]

    return call(
        final_kernel,
        (shape(2, 3, 2, width // total, width), shape(2, cols, cols)),
        (places, directions, slice_group, block_group, *tables, *pieces), scalars=4,
        scratch=(pltpu.VMEM((6 * width, width), jnp.float32),
                 pltpu.VMEM((6 * 128, width), jnp.float32)),
        flops=36 * cols * width * width)


def solution(mesh):
    return jax.shard_map(
        program,
        mesh=mesh,
        in_specs=(
            P("cfg", None, None, "space", None),
            P("cfg", None, None, None, None, "space"),
            P(),
            P(),
            P("cfg", None, "space"),
            P("space"),
        ),
        out_specs=(P("cfg", None, None, "space", None), P("cfg", "space", None)),
        check_vma=False,
    )
```

```python
import functools

import jax
import jax.numpy as jnp
import numpy as np
from jax import lax
from jax.experimental import pallas as pl
from jax.experimental.pallas import tpu as pltpu
from jax.sharding import PartitionSpec as P

LZ = 16
VMEM = pl.BlockSpec(memory_space=pltpu.VMEM)
SMEM = pl.BlockSpec(memory_space=pltpu.SMEM)
NT_DIMS = (((1,), (1,)), ((), ()))
NN_DIMS = (((1,), (0,)), ((), ()))


def split(value):
    high = value.astype(jnp.bfloat16)
    low = (value - high.astype(jnp.float32)).astype(jnp.bfloat16)
    return high, low


def dot3(left, right, dims):
    dot = functools.partial(
        lax.dot_general, dimension_numbers=dims, preferred_element_type=jnp.float32
    )
    return dot(left[0], right[0]) + dot(left[0], right[1]) + dot(left[1], right[0])


def store_left(load, left_ref):
    for colour in range(3):
        real, imag = load(0, colour), load(1, colour)
        count, width = 2 * real.shape[0], real.shape[1]
        at = slice(colour * count, (colour + 1) * count)
        for i, pair in enumerate(((real, imag), (imag, -real))):
            for level, value in enumerate(split(jnp.concatenate(pair, axis=0).T)):
                left_ref[level, i * width : (i + 1) * width, at] = value


def add(total, term):
    return term if total is None else total + term


def store_right(right_ref, row, sites, sources):
    width = right_ref.shape[2]
    coefs = []
    for coef, base, _, turned in sources:
        wide = [jnp.broadcast_to(coef[:, base + j : base + j + 1], (LZ, 128)) for j in range(18)]
        if turned:
            order = [(b * 6 + a * 2, a, b) for a in range(3) for b in range(3)]
            wide = [w for at, _, _ in order for w in (-wide[at], wide[at + 1])]
        coefs.append(wide)
    for lanes in range(0, width, 128):
        cut = slice(lanes, lanes + 128)
        fields = []
        for _, _, field, _ in sources:
            real, imag = field(cut)
            fields.append(([r + i for r, i in zip(real, imag)], [r - i for r, i in zip(real, imag)]))
        for a in range(3):
            alpha = beta = None
            for wide, (plus, minus) in zip(coefs, fields):
                for b in range(3):
                    real, imag = wide[a * 6 + b * 2], wide[a * 6 + b * 2 + 1]
                    alpha = add(add(alpha, real * plus[b]), imag * minus[b])
                    beta = add(add(beta, imag * plus[b]), -(real * minus[b]))
            for part, value in enumerate((alpha, beta)):
                at = (a * 2 + part) * sites + row * LZ
                if value is None:
                    value = jnp.zeros((LZ, 128), jnp.float32)
                high, low = split(value)
                right_ref[0, at : at + LZ, cut] = high
                right_ref[1, at : at + LZ, cut] = low


def row_of(v_ref, row, turn=False):
    def load(cut):
        at = slice(row * LZ, (row + 1) * LZ)
        parts = [[v_ref[p, c, at, cut] for c in range(3)] for p in range(2)]
        if turn:
            parts = [[pltpu.roll(x, LZ - 1, 0) for x in part] for part in parts]
        return parts

    return load


def adjoint_rows(rows):
    out = []
    for a in range(3):
        for b in range(3):
            at = b * 6 + a * 2
            out += [-rows[at : at + 1], rows[at + 1 : at + 2]]
    return jnp.concatenate(out, axis=0)


def of_time(ref, odd):
    count = ref.shape[0] // 2
    return 0.5 * jnp.where(odd == 0, ref[:count], ref[count:])


def contract(left_ref, right_ref):
    left = (left_ref[0], left_ref[1])
    right = (right_ref[0], right_ref[1])
    both = dot3(left, right, NN_DIMS)
    width = right_ref.shape[2]
    return both[:width] - both[width:].T


def own_kernel(place_ref, v0_ref, v1_ref, halo_ref, link_ref, out_ref, left_ref, right_ref,
               coef_ref):
    odd = (place_ref[0] // 2) % 2
    coef_ref[:54, :] = of_time(link_ref, odd)
    store_left(lambda p, c: jnp.concatenate([v0_ref[p, c], v1_ref[p, c]], axis=0), left_ref)
    coef = coef_ref[...].T
    half = v0_ref.shape[2] // LZ

    def at(row, turn=False):
        if row == 2 * half:
            return row_of(halo_ref, 0)
        return row_of((v0_ref, v1_ref)[row // half], row % half, turn)

    for row in range(2 * half):
        here = coef[row * LZ : (row + 1) * LZ]
        sites = 2 * half * LZ
        store_right(right_ref.at[0], row, sites, [(here, 18, at(row + 1), False)])
        store_right(right_ref.at[1], row, sites, [(here, 36, at(row, True), False)])
    for i in range(2):
        out_ref[i] = contract(left_ref, right_ref.at[i])


def chunk(va_ref, vb_ref, vc_ref, coef, start, ahead, left_ref, right_ref):
    sites = vb_ref.shape[2]
    store_left(lambda p, c: vb_ref[p, c], left_ref)
    for row in range(sites // LZ):
        here = coef[start + row * LZ : start + (row + 1) * LZ]
        along = [(here, 56, row_of(va_ref, row), False), (here, 80, row_of(vc_ref, row), False)]
        store_right(right_ref.at[0], row, sites, along)
        store_right(right_ref.at[1], row, sites, ahead(row, here))
        store_right(right_ref.at[2], row, sites, [(here, 36, row_of(vb_ref, row, True), False)])
    return [contract(left_ref, right_ref.at[i]) for i in range(3)]


def first_kernel(place_ref, va_ref, vb_ref, vc_ref, link_a, link_b, link_c, own_ref,
                 out_ref, turned_ref, left_ref, right_ref, coef_ref):
    width = vb_ref.shape[3]
    rows = vb_ref.shape[2] // LZ
    odd = (place_ref[0] // 2) % 2
    coef_ref[:54, :] = of_time(link_b, odd)
    there = coef_ref[:18, :]
    before = adjoint_rows(of_time(link_a, odd)[:18])
    after = adjoint_rows(of_time(link_c, odd)[:18])
    coef_ref[56:74, :] = jnp.where(odd == 0, before, there)
    coef_ref[80:98, :] = jnp.where(odd == 0, there, after)
    turned_ref[...] = coef_ref[...].T
    coef = turned_ref[...]

    def ahead(row, here):
        return [(here, 18, row_of(vb_ref, row + 1), False)] if row + 1 < rows else []

    sums = chunk(va_ref, vb_ref, vc_ref, coef, 0, ahead, left_ref, right_ref)
    for i, value in enumerate(sums):
        out_ref[i * width : (i + 1) * width, :] = value + own_ref[i - 1] if i else value


def last_kernel(place_ref, va_ref, vb_ref, vc_ref, before_ref, halo_ref, turned_ref, first_ref,
                keep_ref, send_ref, left_ref, right_ref, total_ref):
    sites, width = vb_ref.shape[2], vb_ref.shape[3]
    rows = sites // LZ
    coef = turned_ref[...]

    def ahead(row, here):
        field = row_of(vb_ref, row + 1) if row + 1 < rows else row_of(halo_ref, 0)
        out = [(here, 18, field, False)]
        if row == 0:
            out.append((coef[sites - LZ : sites], 18, row_of(before_ref, rows - 1), True))
        return out

    sums = chunk(va_ref, vb_ref, vc_ref, coef, sites, ahead, left_ref, right_ref)
    for i, value in enumerate(sums):
        at = slice(i * width, (i + 1) * width)
        total_ref[at, :] = value + first_ref[at, :]
    core = place_ref[0] % 2
    half = 3 * width // 2
    keep_ref[...] = total_ref[pl.ds(pl.multiple_of(core * half, 8), half), :]
    send_ref[...] = total_ref[pl.ds(pl.multiple_of((1 - core) * half, 8), half), :]


def spread_kernel(place_ref, keep_ref, got_ref, *refs):
    outs, total_ref = refs[:-1], refs[-1]
    total_ref[...] = keep_ref[...] + got_ref[...]
    count = len(outs)
    size = outs[0].shape[0]
    pair = place_ref[0] // 4
    for d in range(count):
        at = lax.rem(pair + d, count) * size
        outs[d][...] = total_ref[pl.ds(pl.multiple_of(at, 8), size), :]


def sum_kernel(*refs):
    total = refs[0][...]
    for ref in refs[1:-1]:
        total = total + ref[...]
    refs[-1][...] = total


def table_kernel(p_ref, b_high, b_low, q_high, q_low):
    width = p_ref.shape[2] // 4
    cols = p_ref.shape[1]

    def spin(part, a):
        return p_ref[part, :, a * width : (a + 1) * width]

    m = [0.5 * (spin(0, a) - spin(1, a)) for a in (2, 3)]
    s = [0.5 * (spin(0, a) + spin(1, a)) for a in (2, 3)]
    pieces = {"m0": split(m[0]), "m1": split(m[1]), "s0": split(s[0]), "s1": split(s[1])}
    table = (
        ("+m1", "+s1", "+m0", "+s0"),
        ("+s1", "-m1", "-s0", "+m0"),
        ("+m0", "+s0", "-m1", "-s1"),
        ("-s1", "+m1", "-s0", "+m0"),
        ("+m1", "+s1", "-m0", "-s0"),
        ("-s0", "+m0", "+s1", "-m1"),
    )
    for k, names in enumerate(table):
        for j, name in enumerate(names):
            high, low = pieces[name[1:]]
            if name[0] == "-":
                high, low = -high, -low
            where = (slice(j * cols, (j + 1) * cols), slice(k * width, (k + 1) * width))
            b_high[where] = high
            b_low[where] = low
    for a in range(2):
        for part in range(2):
            high, low = split(spin(part, a))
            at = (a * 2 + part) * width
            q_high[:, at : at + width] = high
            q_low[:, at : at + width] = low


def take(ref, at, rows):
    if rows % 8 == 0:
        return ref[pl.ds(pl.multiple_of(at, 8), rows), :]
    inner = lax.rem(at, 8)
    tile = ref[pl.ds(pl.multiple_of(at - inner, 8), 8), :]
    return pltpu.roll(tile, lax.rem(8 - inner, 8), 0)[:rows]


def final_kernel(place_ref, direct_ref, slice_ref, block_ref, b_high, b_low, q_high, q_low,
                 *refs):
    count = (len(refs) - 4) // 4
    pieces = refs[: 4 * count]
    elem_ref, out_ref, all_ref, turn_ref = refs[4 * count :]
    size, width = pieces[0].shape
    place = place_ref[0]
    core = place % 2
    odd = (place // 2) % 2
    pair = place // 4
    half = 3 * width // 2
    for side in range(2):
        for other in range(2):
            for d in range(count):
                time = (odd + other) % 2
                base = (time * 2 + (core + side) % 2) * half
                at = base + lax.rem(pair - d + count, count) * size
                piece = pieces[(side * 2 + other) * count + d]
                all_ref[pl.ds(pl.multiple_of(at, 8), size), :] = piece[...]
    rows = elem_ref.shape[3]
    first = place * rows
    lane = pl.multiple_of((first // 128) * 128, 128)
    for i in range(6):
        block = all_ref[i * width : (i + 1) * width, pl.ds(lane, 128)]
        turn_ref[i * 128 : (i + 1) * 128, :] = block.T
    inner = lax.rem(first, 128)
    for g in range(2):
        time = jnp.where(slice_ref[0] == g, 0, 1)
        for k in range(3):
            which = time * 3 + direct_ref[k]
            row = take(all_ref, which * width + first, rows)
            col = take(turn_ref, which * 128 + inner, rows)
            elem_ref[g, k, 0] = 0.5 * (row - col)
            elem_ref[g, k, 1] = 0.5 * (row + col)
    time = jnp.where(slice_ref[0] == block_ref[0], 0, 1)
    turned = None
    for k in range(3):
        at = pl.multiple_of((time * 3 + direct_ref[k]) * width, 8)
        parts = split(all_ref[pl.ds(at, width), :])
        one = slice(k * width, (k + 1) * width)
        two = slice((3 + k) * width, (4 + k) * width)
        term = dot3((b_high[:, one], b_low[:, one]), parts, NT_DIMS) + dot3(
            (b_high[:, two], b_low[:, two]), parts, NN_DIMS
        )
        turned = term if turned is None else turned + term
    cols = q_high.shape[0]
    y = [turned[j * cols : (j + 1) * cols] for j in range(4)]
    same = split(jnp.concatenate([y[0], y[1], y[2], y[3]], axis=1))
    cross = split(jnp.concatenate([y[1], -y[0], y[3], -y[2]], axis=1))
    q = (q_high[...], q_low[...])
    out_ref[0] = dot3(q, cross, NT_DIMS) - dot3(cross, q, NT_DIMS)
    out_ref[1] = -(dot3(q, same, NT_DIMS) + dot3(same, q, NT_DIMS))


def shape(*dims, dtype=jnp.float32):
    return jax.ShapeDtypeStruct(dims, dtype)


def size_of(x):
    return x.size * jnp.dtype(x.dtype).itemsize


def call(kernel, out, operands, scalars=0, scratch=(), flops=0):
    outs = jax.tree.leaves(out)
    moved = sum(size_of(x) for x in list(operands) + outs)
    held = sum(int(np.prod(x.shape)) * jnp.dtype(x.dtype).itemsize for x in scratch)
    limit = moved + held + (4 << 20)
    return pl.pallas_call(
        kernel,
        out_shape=out,
        in_specs=[SMEM] * scalars + [VMEM] * (len(operands) - scalars),
        out_specs=jax.tree.map(lambda _: VMEM, out),
        scratch_shapes=list(scratch),
        cost_estimate=pl.CostEstimate(flops=flops, bytes_accessed=moved, transcendentals=0),
        compiler_params=pltpu.CompilerParams(vmem_limit_bytes=limit),
    )(*operands)


def program(vectors, links, directions, slice_group, peram, block_group):
    total = lax.axis_size("space")
    place = lax.axis_index("space")
    places = jnp.full((1,), place, jnp.int32)
    sites, width = vectors.shape[3], vectors.shape[4]
    pairs = total // 4
    odd = (place // 2) % 2

    def send(value, where):
        route = []
        for i in range(total):
            pair, o, core = where(i // 4, (i // 2) % 2, i % 2)
            route.append((i, ((pair % pairs) * 2 + o) * 2 + core))
        return lax.ppermute(value, "space", route)

    partner = lambda pair, o, core: (pair, 1 - o, core)
    twin = lambda pair, o, core: (pair, o, 1 - core)
    along = lambda pair, o, core: (pair + (1 if o else -1), o, core)

    def shift(d):
        return lambda pair, o, core: (pair + d, o, core)

    flat = links.transpose(0, 1, 3, 4, 2, 5).reshape(links.shape[0] * 54, sites)
    part = sites // 2

    def cut(time, i):
        block = (1,) + vectors.shape[1:3] + (part, width)
        return lax.dynamic_slice(vectors, (time, 0, 0, i * part, 0), block)[0]

    mine = [cut(odd, i) for i in range(2)]
    theirs = [cut(1 - odd, i) for i in range(2)]
    vec_b, vec_c = [], []
    for i in range(2):
        vec_b.append(send(theirs[i], partner))
        vec_c.append(send(mine[i], along))
    link_b = send(flat, partner)
    link_c = send(flat, along)
    halo_a = send(mine[0][:, :, :LZ], twin)
    halo_b = send(vec_b[0][:, :, :LZ], twin)

    def left(n):
        return pltpu.VMEM((2, 2 * width, 6 * n), jnp.bfloat16)

    def right(count, n):
        return pltpu.VMEM((count, 2, 6 * n, width), jnp.bfloat16)

    coef = pltpu.VMEM((128, sites), jnp.float32)
    work = 6 * 6 * sites * 2 * width * width
    own = call(own_kernel, shape(2, width, width), (places, *mine, halo_a, flat), scalars=1,
               scratch=(left(sites), right(2, sites), coef), flops=2 * work)
    cols = peram.shape[2]
    turned = jnp.swapaxes(peram, 1, 2)
    bf16 = jnp.bfloat16
    tables = call(
        table_kernel,
        (shape(4 * cols, 6 * width, dtype=bf16),) * 2
        + (shape(cols, 4 * width, dtype=bf16),) * 2,
        (turned,))
    half = 3 * width // 2
    first, turned = call(
        first_kernel, (shape(3 * width, width), shape(sites, 128)),
        (places, mine[0], vec_b[0], vec_c[0], flat, link_b, link_c, own), scalars=1,
        scratch=(left(part), right(3, part), coef), flops=2 * work)
    keep, give = call(
        last_kernel, (shape(half, width),) * 2,
        (places, mine[1], vec_b[1], vec_c[1], vec_b[0], halo_b, turned, first), scalars=1,
        scratch=(left(part), right(3, part), pltpu.VMEM((3 * width, width), jnp.float32)),
        flops=2 * work)
    got = send(give, twin)
    size = half // pairs
    spread = call(spread_kernel, (shape(size, width),) * pairs, (places, keep, got), scalars=1,
                  scratch=(pltpu.VMEM((half, width), jnp.float32),))
    parts = [spread[0]] + [send(spread[d], shift(d)) for d in range(1, pairs)]
    shard = call(sum_kernel, shape(size, width), parts)
    here = [shard] + [send(shard, shift(d)) for d in range(1, pairs)]
    there = [send(x, partner) for x in here]
    pieces = here + there
    pieces = pieces + [send(x, twin) for x in pieces]

    return call(
        final_kernel,
        (shape(2, 3, 2, width // total, width), shape(2, cols, cols)),
        (places, directions, slice_group, block_group, *tables, *pieces), scalars=4,
        scratch=(pltpu.VMEM((6 * width, width), jnp.float32),
                 pltpu.VMEM((6 * 128, width), jnp.float32)),
        flops=36 * cols * width * width)


def solution(mesh):
    return jax.shard_map(
        program,
        mesh=mesh,
        in_specs=(
            P("cfg", None, None, "space", None),
            P("cfg", None, None, None, None, "space"),
            P(),
            P(),
            P("cfg", None, "space"),
            P("space"),
        ),
        out_specs=(P("cfg", None, None, "space", None), P("cfg", "space", None)),
        check_vma=False,
    )
```

```python
import functools

import jax
import jax.numpy as jnp
import numpy as np
from jax import lax
from jax.experimental import pallas as pl
from jax.experimental.pallas import tpu as pltpu
from jax.sharding import PartitionSpec as P

LZ = 16
VMEM = pl.BlockSpec(memory_space=pltpu.VMEM)
SMEM = pl.BlockSpec(memory_space=pltpu.SMEM)
NT_DIMS = (((1,), (1,)), ((), ()))
NN_DIMS = (((1,), (0,)), ((), ()))


def split(value):
    high = value.astype(jnp.bfloat16)
    low = (value - high.astype(jnp.float32)).astype(jnp.bfloat16)
    return high, low


def dot3(left, right, dims):
    dot = functools.partial(
        lax.dot_general, dimension_numbers=dims, preferred_element_type=jnp.float32
    )
    return dot(left[0], right[0]) + dot(left[0], right[1]) + dot(left[1], right[0])


def store_left(load, left_ref):
    for colour in range(3):
        real, imag = load(0, colour), load(1, colour)
        count, width = 2 * real.shape[0], real.shape[1]
        at = slice(colour * count, (colour + 1) * count)
        for i, pair in enumerate(((real, imag), (imag, -real))):
            for level, value in enumerate(split(jnp.concatenate(pair, axis=0).T)):
                left_ref[level, i * width : (i + 1) * width, at] = value


def add(total, term):
    return term if total is None else total + term


def store_right(right_ref, row, sites, sources):
    width = right_ref.shape[2]
    coefs = []
    for coef, base, _, turned in sources:
        wide = [jnp.broadcast_to(coef[:, base + j : base + j + 1], (LZ, 128)) for j in range(18)]
        if turned:
            order = [(b * 6 + a * 2, a, b) for a in range(3) for b in range(3)]
            wide = [w for at, _, _ in order for w in (-wide[at], wide[at + 1])]
        coefs.append(wide)
    for lanes in range(0, width, 128):
        cut = slice(lanes, lanes + 128)
        fields = []
        for _, _, field, _ in sources:
            real, imag = field(cut)
            fields.append(([r + i for r, i in zip(real, imag)], [r - i for r, i in zip(real, imag)]))
        for a in range(3):
            alpha = beta = None
            for wide, (plus, minus) in zip(coefs, fields):
                for b in range(3):
                    real, imag = wide[a * 6 + b * 2], wide[a * 6 + b * 2 + 1]
                    alpha = add(add(alpha, real * plus[b]), imag * minus[b])
                    beta = add(add(beta, imag * plus[b]), -(real * minus[b]))
            for part, value in enumerate((alpha, beta)):
                at = (a * 2 + part) * sites + row * LZ
                if value is None:
                    value = jnp.zeros((LZ, 128), jnp.float32)
                high, low = split(value)
                right_ref[0, at : at + LZ, cut] = high
                right_ref[1, at : at + LZ, cut] = low


def row_of(v_ref, row, turn=False):
    def load(cut):
        at = slice(row * LZ, (row + 1) * LZ)
        parts = [[v_ref[p, c, at, cut] for c in range(3)] for p in range(2)]
        if turn:
            parts = [[pltpu.roll(x, LZ - 1, 0) for x in part] for part in parts]
        return parts

    return load


def adjoint_rows(rows):
    out = []
    for a in range(3):
        for b in range(3):
            at = b * 6 + a * 2
            out += [-rows[at : at + 1], rows[at + 1 : at + 2]]
    return jnp.concatenate(out, axis=0)


def of_time(ref, odd):
    count = ref.shape[0] // 2
    return 0.5 * jnp.where(odd == 0, ref[:count], ref[count:])


def contract(left_ref, right_ref):
    left = (left_ref[0], left_ref[1])
    right = (right_ref[0], right_ref[1])
    both = dot3(left, right, NN_DIMS)
    width = right_ref.shape[2]
    return both[:width] - both[width:].T


def own_kernel(place_ref, v0_ref, v1_ref, halo_ref, link_ref, out_ref, left_ref, right_ref,
               coef_ref):
    odd = (place_ref[0] // 2) % 2
    coef_ref[:54, :] = of_time(link_ref, odd)
    store_left(lambda p, c: jnp.concatenate([v0_ref[p, c], v1_ref[p, c]], axis=0), left_ref)
    coef = coef_ref[...].T
    half = v0_ref.shape[2] // LZ

    def at(row, turn=False):
        if row == 2 * half:
            return row_of(halo_ref, 0)
        return row_of((v0_ref, v1_ref)[row // half], row % half, turn)

    for row in range(2 * half):
        here = coef[row * LZ : (row + 1) * LZ]
        sites = 2 * half * LZ
        store_right(right_ref.at[0], row, sites, [(here, 18, at(row + 1), False)])
        store_right(right_ref.at[1], row, sites, [(here, 36, at(row, True), False)])
    for i in range(2):
        out_ref[i] = contract(left_ref, right_ref.at[i])


def chunk(va_ref, vb_ref, vc_ref, coef, start, ahead, left_ref, right_ref):
    sites = vb_ref.shape[2]
    store_left(lambda p, c: vb_ref[p, c], left_ref)
    for row in range(sites // LZ):
        here = coef[start + row * LZ : start + (row + 1) * LZ]
        along = [(here, 56, row_of(va_ref, row), False), (here, 80, row_of(vc_ref, row), False)]
        store_right(right_ref.at[0], row, sites, along)
        store_right(right_ref.at[1], row, sites, ahead(row, here))
        store_right(right_ref.at[2], row, sites, [(here, 36, row_of(vb_ref, row, True), False)])
    return [contract(left_ref, right_ref.at[i]) for i in range(3)]


def first_kernel(place_ref, va_ref, vb_ref, vc_ref, link_a, link_b, link_c, own_ref,
                 out_ref, turned_ref, left_ref, right_ref, coef_ref):
    width = vb_ref.shape[3]
    rows = vb_ref.shape[2] // LZ
    odd = (place_ref[0] // 2) % 2
    coef_ref[:54, :] = of_time(link_b, odd)
    there = coef_ref[:18, :]
    before = adjoint_rows(of_time(link_a, odd)[:18])
    after = adjoint_rows(of_time(link_c, odd)[:18])
    coef_ref[56:74, :] = jnp.where(odd == 0, before, there)
    coef_ref[80:98, :] = jnp.where(odd == 0, there, after)
    turned_ref[...] = coef_ref[...].T
    coef = turned_ref[...]

    def ahead(row, here):
        return [(here, 18, row_of(vb_ref, row + 1), False)] if row + 1 < rows else []

    sums = chunk(va_ref, vb_ref, vc_ref, coef, 0, ahead, left_ref, right_ref)
    for i, value in enumerate(sums):
        out_ref[i * width : (i + 1) * width, :] = value + own_ref[i - 1] if i else value


def last_kernel(place_ref, va_ref, vb_ref, vc_ref, before_ref, halo_ref, turned_ref, first_ref,
                keep_ref, send_ref, left_ref, right_ref, total_ref):
    sites, width = vb_ref.shape[2], vb_ref.shape[3]
    rows = sites // LZ
    coef = turned_ref[...]

    def ahead(row, here):
        field = row_of(vb_ref, row + 1) if row + 1 < rows else row_of(halo_ref, 0)
        out = [(here, 18, field, False)]
        if row == 0:
            out.append((coef[sites - LZ : sites], 18, row_of(before_ref, rows - 1), True))
        return out

    sums = chunk(va_ref, vb_ref, vc_ref, coef, sites, ahead, left_ref, right_ref)
    for i, value in enumerate(sums):
        at = slice(i * width, (i + 1) * width)
        total_ref[at, :] = value + first_ref[at, :]
    core = place_ref[0] % 2
    half = 3 * width // 2
    keep_ref[...] = total_ref[pl.ds(pl.multiple_of(core * half, 8), half), :]
    send_ref[...] = total_ref[pl.ds(pl.multiple_of((1 - core) * half, 8), half), :]


def part_row(pair, d, count, size):
    if count == 4:
        return (((pair % 2) ^ (d // 2)) * 2 + d % 2) * size
    return lax.rem(pair + count - d, count) * size


def spread_kernel(place_ref, keep_ref, got_ref, *refs):
    outs, total_ref = refs[:-1], refs[-1]
    total_ref[...] = keep_ref[...] + got_ref[...]
    count = len(outs)
    size = outs[0].shape[0]
    pair = place_ref[0] // 4
    for d in range(count):
        at = part_row(pair, d if count == 4 else -d, count, size)
        outs[d][...] = total_ref[pl.ds(pl.multiple_of(at, 8), size), :]


def sum_kernel(*refs):
    total = refs[0][...]
    for ref in refs[1:-1]:
        total = total + ref[...]
    refs[-1][...] = total


def table_kernel(p_ref, b_high, b_low, q_high, q_low):
    width = p_ref.shape[2] // 4
    cols = p_ref.shape[1]

    def spin(part, a):
        return p_ref[part, :, a * width : (a + 1) * width]

    m = [0.5 * (spin(0, a) - spin(1, a)) for a in (2, 3)]
    s = [0.5 * (spin(0, a) + spin(1, a)) for a in (2, 3)]
    pieces = {"m0": split(m[0]), "m1": split(m[1]), "s0": split(s[0]), "s1": split(s[1])}
    table = (
        ("+m1", "+s1", "+m0", "+s0"),
        ("+s1", "-m1", "-s0", "+m0"),
        ("+m0", "+s0", "-m1", "-s1"),
        ("-s1", "+m1", "-s0", "+m0"),
        ("+m1", "+s1", "-m0", "-s0"),
        ("-s0", "+m0", "+s1", "-m1"),
    )
    for k, names in enumerate(table):
        for j, name in enumerate(names):
            high, low = pieces[name[1:]]
            if name[0] == "-":
                high, low = -high, -low
            where = (slice(j * cols, (j + 1) * cols), slice(k * width, (k + 1) * width))
            b_high[where] = high
            b_low[where] = low
    for a in range(2):
        for part in range(2):
            high, low = split(spin(part, a))
            at = (a * 2 + part) * width
            q_high[:, at : at + width] = high
            q_low[:, at : at + width] = low


def take(ref, at, rows):
    if rows % 8 == 0:
        return ref[pl.ds(pl.multiple_of(at, 8), rows), :]
    inner = lax.rem(at, 8)
    tile = ref[pl.ds(pl.multiple_of(at - inner, 8), 8), :]
    return pltpu.roll(tile, lax.rem(8 - inner, 8), 0)[:rows]


def final_kernel(place_ref, direct_ref, slice_ref, block_ref, b_high, b_low, q_high, q_low,
                 *refs):
    count = (len(refs) - 4) // 4
    pieces = refs[: 4 * count]
    elem_ref, out_ref, all_ref, turn_ref = refs[4 * count :]
    size, width = pieces[0].shape
    place = place_ref[0]
    core = place % 2
    odd = (place // 2) % 2
    pair = place // 4
    half = 3 * width // 2
    for side in range(2):
        for other in range(2):
            for d in range(count):
                time = (odd + other) % 2
                base = (time * 2 + (core + side) % 2) * half
                at = base + part_row(pair, d, count, size)
                piece = pieces[(side * 2 + other) * count + d]
                all_ref[pl.ds(pl.multiple_of(at, 8), size), :] = piece[...]
    rows = elem_ref.shape[3]
    first = place * rows
    lane = pl.multiple_of((first // 128) * 128, 128)
    for i in range(6):
        block = all_ref[i * width : (i + 1) * width, pl.ds(lane, 128)]
        turn_ref[i * 128 : (i + 1) * 128, :] = block.T
    inner = lax.rem(first, 128)
    for g in range(2):
        time = jnp.where(slice_ref[0] == g, 0, 1)
        for k in range(3):
            which = time * 3 + direct_ref[k]
            row = take(all_ref, which * width + first, rows)
            col = take(turn_ref, which * 128 + inner, rows)
            elem_ref[g, k, 0] = 0.5 * (row - col)
            elem_ref[g, k, 1] = 0.5 * (row + col)
    time = jnp.where(slice_ref[0] == block_ref[0], 0, 1)
    turned = None
    for k in range(3):
        at = pl.multiple_of((time * 3 + direct_ref[k]) * width, 8)
        parts = split(all_ref[pl.ds(at, width), :])
        one = slice(k * width, (k + 1) * width)
        two = slice((3 + k) * width, (4 + k) * width)
        term = dot3((b_high[:, one], b_low[:, one]), parts, NT_DIMS) + dot3(
            (b_high[:, two], b_low[:, two]), parts, NN_DIMS
        )
        turned = term if turned is None else turned + term
    cols = q_high.shape[0]
    y = [turned[j * cols : (j + 1) * cols] for j in range(4)]
    same = split(jnp.concatenate([y[0], y[1], y[2], y[3]], axis=1))
    cross = split(jnp.concatenate([y[1], -y[0], y[3], -y[2]], axis=1))
    q = (q_high[...], q_low[...])
    out_ref[0] = dot3(q, cross, NT_DIMS) - dot3(cross, q, NT_DIMS)
    out_ref[1] = -(dot3(q, same, NT_DIMS) + dot3(same, q, NT_DIMS))


def shape(*dims, dtype=jnp.float32):
    return jax.ShapeDtypeStruct(dims, dtype)


def size_of(x):
    return x.size * jnp.dtype(x.dtype).itemsize


def call(kernel, out, operands, scalars=0, scratch=(), flops=0):
    outs = jax.tree.leaves(out)
    moved = sum(size_of(x) for x in list(operands) + outs)
    held = sum(int(np.prod(x.shape)) * jnp.dtype(x.dtype).itemsize for x in scratch)
    limit = moved + held + (4 << 20)
    return pl.pallas_call(
        kernel,
        out_shape=out,
        in_specs=[SMEM] * scalars + [VMEM] * (len(operands) - scalars),
        out_specs=jax.tree.map(lambda _: VMEM, out),
        scratch_shapes=list(scratch),
        cost_estimate=pl.CostEstimate(flops=flops, bytes_accessed=moved, transcendentals=0),
        compiler_params=pltpu.CompilerParams(vmem_limit_bytes=limit),
    )(*operands)


def program(vectors, links, directions, slice_group, peram, block_group):
    total = lax.axis_size("space")
    place = lax.axis_index("space")
    places = jnp.full((1,), place, jnp.int32)
    sites, width = vectors.shape[3], vectors.shape[4]
    pairs = total // 4
    odd = (place // 2) % 2

    def send(value, where):
        route = []
        for i in range(total):
            pair, o, core = where(i // 4, (i // 2) % 2, i % 2)
            route.append((i, ((pair % pairs) * 2 + o) * 2 + core))
        return lax.ppermute(value, "space", route)

    partner = lambda pair, o, core: (pair, 1 - o, core)
    twin = lambda pair, o, core: (pair, o, 1 - core)
    along = lambda pair, o, core: (pair + (1 if o else -1), o, core)

    def shift(d):
        return lambda pair, o, core: (pair + d, o, core)

    flat = links.transpose(0, 1, 3, 4, 2, 5).reshape(links.shape[0] * 54, sites)
    part = sites // 2

    def cut(time, i):
        block = (1,) + vectors.shape[1:3] + (part, width)
        return lax.dynamic_slice(vectors, (time, 0, 0, i * part, 0), block)[0]

    mine = [cut(odd, i) for i in range(2)]
    theirs = [cut(1 - odd, i) for i in range(2)]
    vec_b, vec_c = [], []
    for i in range(2):
        vec_b.append(send(theirs[i], partner))
        vec_c.append(send(mine[i], along))
    link_b = send(flat, partner)
    link_c = send(flat, along)
    halo_a = send(mine[0][:, :, :LZ], twin)
    halo_b = send(vec_b[0][:, :, :LZ], twin)

    def left(n):
        return pltpu.VMEM((2, 2 * width, 6 * n), jnp.bfloat16)

    def right(count, n):
        return pltpu.VMEM((count, 2, 6 * n, width), jnp.bfloat16)

    coef = pltpu.VMEM((128, sites), jnp.float32)
    work = 6 * 6 * sites * 2 * width * width
    own = call(own_kernel, shape(2, width, width), (places, *mine, halo_a, flat), scalars=1,
               scratch=(left(sites), right(2, sites), coef), flops=2 * work)
    cols = peram.shape[2]
    turned = jnp.swapaxes(peram, 1, 2)
    bf16 = jnp.bfloat16
    tables = call(
        table_kernel,
        (shape(4 * cols, 6 * width, dtype=bf16),) * 2
        + (shape(cols, 4 * width, dtype=bf16),) * 2,
        (turned,))
    half = 3 * width // 2
    first, turned = call(
        first_kernel, (shape(3 * width, width), shape(sites, 128)),
        (places, mine[0], vec_b[0], vec_c[0], flat, link_b, link_c, own), scalars=1,
        scratch=(left(part), right(3, part), coef), flops=2 * work)
    keep, give = call(
        last_kernel, (shape(half, width),) * 2,
        (places, mine[1], vec_b[1], vec_c[1], vec_b[0], halo_b, turned, first), scalars=1,
        scratch=(left(part), right(3, part), pltpu.VMEM((3 * width, width), jnp.float32)),
        flops=2 * work)
    got = send(give, twin)
    size = half // pairs
    spread = call(spread_kernel, (shape(size, width),) * pairs, (places, keep, got), scalars=1,
                  scratch=(pltpu.VMEM((half, width), jnp.float32),))

    def plus(*values):
        return call(sum_kernel, shape(size, width), values)

    if pairs == 4:
        near = lambda pair, o, core: (pair ^ 1, o, core)
        far = lambda pair, o, core: (pair ^ 2, o, core)
        got = [send(spread[2 + i], near) for i in range(2)]
        sums = [plus(spread[i], got[i]) for i in range(2)]
        got = [send(sums[i], far) for i in range(2)]
        done = [plus(sums[i], got[i]) for i in range(2)]
        rest = [send(done[i], near) for i in range(2)]
        here = done + rest
    else:
        parts = [spread[0]] + [send(spread[d], shift(d)) for d in range(1, pairs)]
        shard = plus(*parts)
        here = [shard] + [send(shard, shift(d)) for d in range(1, pairs)]
    there = [send(x, partner) for x in here]
    pieces = here + there
    pieces = pieces + [send(x, twin) for x in pieces]

    return call(
        final_kernel,
        (shape(2, 3, 2, width // total, width), shape(2, cols, cols)),
        (places, directions, slice_group, block_group, *tables, *pieces), scalars=4,
        scratch=(pltpu.VMEM((6 * width, width), jnp.float32),
                 pltpu.VMEM((6 * 128, width), jnp.float32)),
        flops=36 * cols * width * width)


def solution(mesh):
    return jax.shard_map(
        program,
        mesh=mesh,
        in_specs=(
            P("cfg", None, None, "space", None),
            P("cfg", None, None, None, None, "space"),
            P(),
            P(),
            P("cfg", None, "space"),
            P("space"),
        ),
        out_specs=(P("cfg", None, None, "space", None), P("cfg", "space", None)),
        check_vma=False,
    )
```

```python
import functools

import jax
import jax.numpy as jnp
import numpy as np
from jax import lax
from jax.experimental import pallas as pl
from jax.experimental.pallas import tpu as pltpu
from jax.sharding import PartitionSpec as P

LZ = 16
VMEM = pl.BlockSpec(memory_space=pltpu.VMEM)
SMEM = pl.BlockSpec(memory_space=pltpu.SMEM)
NT_DIMS = (((1,), (1,)), ((), ()))
NN_DIMS = (((1,), (0,)), ((), ()))


def split(value):
    high = value.astype(jnp.bfloat16)
    low = (value - high.astype(jnp.float32)).astype(jnp.bfloat16)
    return high, low


def dot3(left, right, dims):
    dot = functools.partial(
        lax.dot_general, dimension_numbers=dims, preferred_element_type=jnp.float32
    )
    return dot(left[0], right[0]) + dot(left[0], right[1]) + dot(left[1], right[0])


def store_left(load, left_ref):
    for colour in range(3):
        real, imag = load(0, colour), load(1, colour)
        count, width = 2 * real.shape[0], real.shape[1]
        at = slice(colour * count, (colour + 1) * count)
        for i, pair in enumerate(((real, imag), (imag, -real))):
            for level, value in enumerate(split(jnp.concatenate(pair, axis=0).T)):
                left_ref[level, i * width : (i + 1) * width, at] = value


def add(total, term):
    return term if total is None else total + term


def store_right(right_ref, row, sites, sources):
    width = right_ref.shape[2]
    coefs = []
    for coef, base, _, turned in sources:
        wide = [jnp.broadcast_to(coef[:, base + j : base + j + 1], (LZ, 128)) for j in range(18)]
        if turned:
            order = [(b * 6 + a * 2, a, b) for a in range(3) for b in range(3)]
            wide = [w for at, _, _ in order for w in (-wide[at], wide[at + 1])]
        coefs.append(wide)
    for lanes in range(0, width, 128):
        cut = slice(lanes, lanes + 128)
        fields = []
        for _, _, field, _ in sources:
            real, imag = field(cut)
            fields.append(([r + i for r, i in zip(real, imag)], [r - i for r, i in zip(real, imag)]))
        for a in range(3):
            alpha = beta = None
            for wide, (plus, minus) in zip(coefs, fields):
                for b in range(3):
                    real, imag = wide[a * 6 + b * 2], wide[a * 6 + b * 2 + 1]
                    alpha = add(add(alpha, real * plus[b]), imag * minus[b])
                    beta = add(add(beta, imag * plus[b]), -(real * minus[b]))
            for part, value in enumerate((alpha, beta)):
                at = (a * 2 + part) * sites + row * LZ
                if value is None:
                    value = jnp.zeros((LZ, 128), jnp.float32)
                high, low = split(value)
                right_ref[0, at : at + LZ, cut] = high
                right_ref[1, at : at + LZ, cut] = low


def row_of(v_ref, row, turn=False):
    def load(cut):
        at = slice(row * LZ, (row + 1) * LZ)
        parts = [[v_ref[p, c, at, cut] for c in range(3)] for p in range(2)]
        if turn:
            parts = [[pltpu.roll(x, LZ - 1, 0) for x in part] for part in parts]
        return parts

    return load


def adjoint_rows(rows):
    out = []
    for a in range(3):
        for b in range(3):
            at = b * 6 + a * 2
            out += [-rows[at : at + 1], rows[at + 1 : at + 2]]
    return jnp.concatenate(out, axis=0)


def of_time(ref, odd):
    count = ref.shape[0] // 2
    return 0.5 * jnp.where(odd == 0, ref[:count], ref[count:])


def contract(left_ref, right_ref):
    left = (left_ref[0], left_ref[1])
    right = (right_ref[0], right_ref[1])
    both = dot3(left, right, NN_DIMS)
    width = right_ref.shape[2]
    return both[:width] - both[width:].T


def own_kernel(place_ref, v0_ref, v1_ref, halo_ref, link_ref, out_ref, left_ref, right_ref,
               coef_ref):
    odd = (place_ref[0] // 2) % 2
    coef_ref[:54, :] = of_time(link_ref, odd)
    store_left(lambda p, c: jnp.concatenate([v0_ref[p, c], v1_ref[p, c]], axis=0), left_ref)
    coef = coef_ref[...].T
    half = v0_ref.shape[2] // LZ

    def at(row, turn=False):
        if row == 2 * half:
            return row_of(halo_ref, 0)
        return row_of((v0_ref, v1_ref)[row // half], row % half, turn)

    for row in range(2 * half):
        here = coef[row * LZ : (row + 1) * LZ]
        sites = 2 * half * LZ
        store_right(right_ref.at[0], row, sites, [(here, 18, at(row + 1), False)])
        store_right(right_ref.at[1], row, sites, [(here, 36, at(row, True), False)])
    for i in range(2):
        out_ref[i] = contract(left_ref, right_ref.at[i])


def chunk(va_ref, vb_ref, vc_ref, coef, start, ahead, left_ref, right_ref):
    sites = vb_ref.shape[2]
    store_left(lambda p, c: vb_ref[p, c], left_ref)
    for row in range(sites // LZ):
        here = coef[start + row * LZ : start + (row + 1) * LZ]
        along = [(here, 56, row_of(va_ref, row), False), (here, 80, row_of(vc_ref, row), False)]
        store_right(right_ref.at[0], row, sites, along)
        store_right(right_ref.at[1], row, sites, ahead(row, here))
        store_right(right_ref.at[2], row, sites, [(here, 36, row_of(vb_ref, row, True), False)])
    return [contract(left_ref, right_ref.at[i]) for i in range(3)]


def first_kernel(place_ref, va_ref, vb_ref, vc_ref, link_a, link_b, link_c, own_ref,
                 out_ref, turned_ref, left_ref, right_ref, coef_ref):
    width = vb_ref.shape[3]
    rows = vb_ref.shape[2] // LZ
    odd = (place_ref[0] // 2) % 2
    coef_ref[:54, :] = of_time(link_b, odd)
    there = coef_ref[:18, :]
    before = adjoint_rows(of_time(link_a, odd)[:18])
    after = adjoint_rows(of_time(link_c, odd))
    coef_ref[56:74, :] = jnp.where(odd == 0, before, there)
    coef_ref[80:98, :] = jnp.where(odd == 0, there, after)
    turned_ref[...] = coef_ref[...].T
    coef = turned_ref[...]

    def ahead(row, here):
        return [(here, 18, row_of(vb_ref, row + 1), False)] if row + 1 < rows else []

    sums = chunk(va_ref, vb_ref, vc_ref, coef, 0, ahead, left_ref, right_ref)
    for i, value in enumerate(sums):
        out_ref[i * width : (i + 1) * width, :] = value + own_ref[i - 1] if i else value


def last_kernel(place_ref, va_ref, vb_ref, vc_ref, before_ref, halo_ref, turned_ref, first_ref,
                keep_ref, send_ref, left_ref, right_ref, total_ref):
    sites, width = vb_ref.shape[2], vb_ref.shape[3]
    rows = sites // LZ
    coef = turned_ref[...]

    def ahead(row, here):
        field = row_of(vb_ref, row + 1) if row + 1 < rows else row_of(halo_ref, 0)
        out = [(here, 18, field, False)]
        if row == 0:
            out.append((coef[sites - LZ : sites], 18, row_of(before_ref, rows - 1), True))
        return out

    sums = chunk(va_ref, vb_ref, vc_ref, coef, sites, ahead, left_ref, right_ref)
    for i, value in enumerate(sums):
        at = slice(i * width, (i + 1) * width)
        total_ref[at, :] = value + first_ref[at, :]
    core = place_ref[0] % 2
    half = 3 * width // 2
    keep_ref[...] = total_ref[pl.ds(pl.multiple_of(core * half, 8), half), :]
    send_ref[...] = total_ref[pl.ds(pl.multiple_of((1 - core) * half, 8), half), :]


def spread_kernel(place_ref, keep_ref, got_ref, *refs):
    outs, total_ref = refs[:-1], refs[-1]
    total_ref[...] = keep_ref[...] + got_ref[...]
    count = len(outs)
    size = outs[0].shape[0]
    pair = place_ref[0] // 4
    for d in range(count):
        at = lax.rem(pair + d, count) * size
        outs[d][...] = total_ref[pl.ds(pl.multiple_of(at, 8), size), :]


def sum_kernel(*refs):
    total = refs[0][...]
    for ref in refs[1:-1]:
        total = total + ref[...]
    refs[-1][...] = total


def table_kernel(p_ref, b_high, b_low, q_high, q_low):
    width = p_ref.shape[2] // 4
    cols = p_ref.shape[1]

    def spin(part, a):
        return p_ref[part, :, a * width : (a + 1) * width]

    m = [0.5 * (spin(0, a) - spin(1, a)) for a in (2, 3)]
    s = [0.5 * (spin(0, a) + spin(1, a)) for a in (2, 3)]
    pieces = {"m0": split(m[0]), "m1": split(m[1]), "s0": split(s[0]), "s1": split(s[1])}
    table = (
        ("+m1", "+s1", "+m0", "+s0"),
        ("+s1", "-m1", "-s0", "+m0"),
        ("+m0", "+s0", "-m1", "-s1"),
        ("-s1", "+m1", "-s0", "+m0"),
        ("+m1", "+s1", "-m0", "-s0"),
        ("-s0", "+m0", "+s1", "-m1"),
    )
    for k, names in enumerate(table):
        for j, name in enumerate(names):
            high, low = pieces[name[1:]]
            if name[0] == "-":
                high, low = -high, -low
            where = (slice(j * cols, (j + 1) * cols), slice(k * width, (k + 1) * width))
            b_high[where] = high
            b_low[where] = low
    for a in range(2):
        for part in range(2):
            high, low = split(spin(part, a))
            at = (a * 2 + part) * width
            q_high[:, at : at + width] = high
            q_low[:, at : at + width] = low


def take(ref, at, rows):
    if rows % 8 == 0:
        return ref[pl.ds(pl.multiple_of(at, 8), rows), :]
    inner = lax.rem(at, 8)
    tile = ref[pl.ds(pl.multiple_of(at - inner, 8), 8), :]
    return pltpu.roll(tile, lax.rem(8 - inner, 8), 0)[:rows]


def final_kernel(place_ref, direct_ref, slice_ref, block_ref, b_high, b_low, q_high, q_low,
                 *refs):
    count = (len(refs) - 4) // 4
    pieces = refs[: 4 * count]
    elem_ref, out_ref, all_ref, turn_ref = refs[4 * count :]
    size, width = pieces[0].shape
    place = place_ref[0]
    core = place % 2
    odd = (place // 2) % 2
    pair = place // 4
    half = 3 * width // 2
    for side in range(2):
        for other in range(2):
            for d in range(count):
                time = (odd + other) % 2
                base = (time * 2 + (core + side) % 2) * half
                at = base + lax.rem(pair - d + count, count) * size
                piece = pieces[(side * 2 + other) * count + d]
                all_ref[pl.ds(pl.multiple_of(at, 8), size), :] = piece[...]
    rows = elem_ref.shape[3]
    first = place * rows
    lane = pl.multiple_of((first // 128) * 128, 128)
    for i in range(6):
        block = all_ref[i * width : (i + 1) * width, pl.ds(lane, 128)]
        turn_ref[i * 128 : (i + 1) * 128, :] = block.T
    inner = lax.rem(first, 128)
    for g in range(2):
        time = jnp.where(slice_ref[0] == g, 0, 1)
        for k in range(3):
            which = time * 3 + direct_ref[k]
            row = take(all_ref, which * width + first, rows)
            col = take(turn_ref, which * 128 + inner, rows)
            elem_ref[g, k, 0] = 0.5 * (row - col)
            elem_ref[g, k, 1] = 0.5 * (row + col)
    time = jnp.where(slice_ref[0] == block_ref[0], 0, 1)
    turned = None
    for k in range(3):
        at = pl.multiple_of((time * 3 + direct_ref[k]) * width, 8)
        parts = split(all_ref[pl.ds(at, width), :])
        one = slice(k * width, (k + 1) * width)
        two = slice((3 + k) * width, (4 + k) * width)
        term = dot3((b_high[:, one], b_low[:, one]), parts, NT_DIMS) + dot3(
            (b_high[:, two], b_low[:, two]), parts, NN_DIMS
        )
        turned = term if turned is None else turned + term
    cols = q_high.shape[0]
    y = [turned[j * cols : (j + 1) * cols] for j in range(4)]
    same = split(jnp.concatenate([y[0], y[1], y[2], y[3]], axis=1))
    cross = split(jnp.concatenate([y[1], -y[0], y[3], -y[2]], axis=1))
    q = (q_high[...], q_low[...])
    out_ref[0] = dot3(q, cross, NT_DIMS) - dot3(cross, q, NT_DIMS)
    out_ref[1] = -(dot3(q, same, NT_DIMS) + dot3(same, q, NT_DIMS))


def shape(*dims, dtype=jnp.float32):
    return jax.ShapeDtypeStruct(dims, dtype)


def size_of(x):
    return x.size * jnp.dtype(x.dtype).itemsize


def call(kernel, out, operands, scalars=0, scratch=(), flops=0):
    outs = jax.tree.leaves(out)
    moved = sum(size_of(x) for x in list(operands) + outs)
    held = sum(int(np.prod(x.shape)) * jnp.dtype(x.dtype).itemsize for x in scratch)
    limit = moved + held + (4 << 20)
    return pl.pallas_call(
        kernel,
        out_shape=out,
        in_specs=[SMEM] * scalars + [VMEM] * (len(operands) - scalars),
        out_specs=jax.tree.map(lambda _: VMEM, out),
        scratch_shapes=list(scratch),
        cost_estimate=pl.CostEstimate(flops=flops, bytes_accessed=moved, transcendentals=0),
        compiler_params=pltpu.CompilerParams(vmem_limit_bytes=limit),
    )(*operands)


def program(vectors, links, directions, slice_group, peram, block_group):
    total = lax.axis_size("space")
    place = lax.axis_index("space")
    places = jnp.full((1,), place, jnp.int32)
    sites, width = vectors.shape[3], vectors.shape[4]
    pairs = total // 4
    odd = (place // 2) % 2

    def send(value, where):
        route = []
        for i in range(total):
            pair, o, core = where(i // 4, (i // 2) % 2, i % 2)
            route.append((i, ((pair % pairs) * 2 + o) * 2 + core))
        return lax.ppermute(value, "space", route)

    partner = lambda pair, o, core: (pair, 1 - o, core)
    twin = lambda pair, o, core: (pair, o, 1 - core)
    along = lambda pair, o, core: (pair + (1 if o else -1), o, core)

    def shift(d):
        return lambda pair, o, core: (pair + d, o, core)

    flat = links.transpose(0, 1, 3, 4, 2, 5).reshape(links.shape[0] * 54, sites)
    part = sites // 2

    def cut(time, i):
        block = (1,) + vectors.shape[1:3] + (part, width)
        return lax.dynamic_slice(vectors, (time, 0, 0, i * part, 0), block)[0]

    mine = [cut(odd, i) for i in range(2)]
    theirs = [cut(1 - odd, i) for i in range(2)]
    vec_b, vec_c = [], []
    for i in range(2):
        vec_b.append(send(theirs[i], partner))
        vec_c.append(send(mine[i], along))
    link_b = send(flat, partner)
    rows = flat.reshape(links.shape[0], 54, sites)[:, :18]
    link_c = send(rows.reshape(links.shape[0] * 18, sites), along)
    halo_a = send(mine[0][:, :, :LZ], twin)
    halo_b = send(vec_b[0][:, :, :LZ], twin)

    def left(n):
        return pltpu.VMEM((2, 2 * width, 6 * n), jnp.bfloat16)

    def right(count, n):
        return pltpu.VMEM((count, 2, 6 * n, width), jnp.bfloat16)

    coef = pltpu.VMEM((128, sites), jnp.float32)
    work = 6 * 6 * sites * 2 * width * width
    own = call(own_kernel, shape(2, width, width), (places, *mine, halo_a, flat), scalars=1,
               scratch=(left(sites), right(2, sites), coef), flops=2 * work)
    cols = peram.shape[2]
    turned = jnp.swapaxes(peram, 1, 2)
    bf16 = jnp.bfloat16
    tables = call(
        table_kernel,
        (shape(4 * cols, 6 * width, dtype=bf16),) * 2
        + (shape(cols, 4 * width, dtype=bf16),) * 2,
        (turned,))
    half = 3 * width // 2
    first, turned = call(
        first_kernel, (shape(3 * width, width), shape(sites, 128)),
        (places, mine[0], vec_b[0], vec_c[0], flat, link_b, link_c, own), scalars=1,
        scratch=(left(part), right(3, part), coef), flops=2 * work)
    keep, give = call(
        last_kernel, (shape(half, width),) * 2,
        (places, mine[1], vec_b[1], vec_c[1], vec_b[0], halo_b, turned, first), scalars=1,
        scratch=(left(part), right(3, part), pltpu.VMEM((3 * width, width), jnp.float32)),
        flops=2 * work)
    got = send(give, twin)
    size = half // pairs
    spread = call(spread_kernel, (shape(size, width),) * pairs, (places, keep, got), scalars=1,
                  scratch=(pltpu.VMEM((half, width), jnp.float32),))

    parts = [spread[0]] + [send(spread[d], shift(d)) for d in range(1, pairs)]
    shard = call(sum_kernel, shape(size, width), parts)
    here = [shard] + [send(shard, shift(d)) for d in range(1, pairs)]
    there = [send(x, partner) for x in here]
    pieces = here + there
    pieces = pieces + [send(x, twin) for x in pieces]

    return call(
        final_kernel,
        (shape(2, 3, 2, width // total, width), shape(2, cols, cols)),
        (places, directions, slice_group, block_group, *tables, *pieces), scalars=4,
        scratch=(pltpu.VMEM((6 * width, width), jnp.float32),
                 pltpu.VMEM((6 * 128, width), jnp.float32)),
        flops=36 * cols * width * width)


def solution(mesh):
    return jax.shard_map(
        program,
        mesh=mesh,
        in_specs=(
            P("cfg", None, None, "space", None),
            P("cfg", None, None, None, None, "space"),
            P(),
            P(),
            P("cfg", None, "space"),
            P("space"),
        ),
        out_specs=(P("cfg", None, None, "space", None), P("cfg", "space", None)),
        check_vma=False,
    )
```

```python
import functools

import jax
import jax.numpy as jnp
import numpy as np
from jax import lax
from jax.experimental import pallas as pl
from jax.experimental.pallas import tpu as pltpu
from jax.sharding import PartitionSpec as P

LZ = 16
VMEM = pl.BlockSpec(memory_space=pltpu.VMEM)
SMEM = pl.BlockSpec(memory_space=pltpu.SMEM)
NT_DIMS = (((1,), (1,)), ((), ()))
NN_DIMS = (((1,), (0,)), ((), ()))


def split(value):
    high = value.astype(jnp.bfloat16)
    low = (value - high.astype(jnp.float32)).astype(jnp.bfloat16)
    return high, low


def dot3(left, right, dims):
    dot = functools.partial(
        lax.dot_general, dimension_numbers=dims, preferred_element_type=jnp.float32
    )
    return dot(left[0], right[0]) + dot(left[0], right[1]) + dot(left[1], right[0])


def store_left(load, left_ref):
    for colour in range(3):
        real, imag = load(0, colour), load(1, colour)
        count, width = 2 * real.shape[0], real.shape[1]
        at = slice(colour * count, (colour + 1) * count)
        for i, pair in enumerate(((real, imag), (imag, -real))):
            for level, value in enumerate(split(jnp.concatenate(pair, axis=0).T)):
                left_ref[level, i * width : (i + 1) * width, at] = value


def add(total, term):
    return term if total is None else total + term


def store_right(right_ref, row, sites, sources):
    width = right_ref.shape[2]
    coefs = []
    for coef, base, _, turned in sources:
        wide = [jnp.broadcast_to(coef[:, base + j : base + j + 1], (LZ, 128)) for j in range(18)]
        if turned:
            order = [(b * 6 + a * 2, a, b) for a in range(3) for b in range(3)]
            wide = [w for at, _, _ in order for w in (-wide[at], wide[at + 1])]
        coefs.append(wide)
    for lanes in range(0, width, 128):
        cut = slice(lanes, lanes + 128)
        fields = []
        for _, _, field, _ in sources:
            real, imag = field(cut)
            fields.append(([r + i for r, i in zip(real, imag)], [r - i for r, i in zip(real, imag)]))
        for a in range(3):
            alpha = beta = None
            for wide, (plus, minus) in zip(coefs, fields):
                for b in range(3):
                    real, imag = wide[a * 6 + b * 2], wide[a * 6 + b * 2 + 1]
                    alpha = add(add(alpha, real * plus[b]), imag * minus[b])
                    beta = add(add(beta, imag * plus[b]), -(real * minus[b]))
            for part, value in enumerate((alpha, beta)):
                at = (a * 2 + part) * sites + row * LZ
                if value is None:
                    value = jnp.zeros((LZ, 128), jnp.float32)
                high, low = split(value)
                right_ref[0, at : at + LZ, cut] = high
                right_ref[1, at : at + LZ, cut] = low


def row_of(v_ref, row, turn=False):
    def load(cut):
        at = slice(row * LZ, (row + 1) * LZ)
        parts = [[v_ref[p, c, at, cut] for c in range(3)] for p in range(2)]
        if turn:
            parts = [[pltpu.roll(x, LZ - 1, 0) for x in part] for part in parts]
        return parts

    return load


def adjoint_rows(rows):
    out = []
    for a in range(3):
        for b in range(3):
            at = b * 6 + a * 2
            out += [-rows[at : at + 1], rows[at + 1 : at + 2]]
    return jnp.concatenate(out, axis=0)


def of_time(ref, odd):
    count = ref.shape[0] // 2
    return 0.5 * jnp.where(odd == 0, ref[:count], ref[count:])


def contract(left_ref, right_ref):
    left = (left_ref[0], left_ref[1])
    right = (right_ref[0], right_ref[1])
    both = dot3(left, right, NN_DIMS)
    width = right_ref.shape[2]
    return both[:width] - both[width:].T


def own_kernel(place_ref, v0_ref, v1_ref, halo_ref, link_ref, out_ref, left_ref, right_ref,
               coef_ref):
    odd = (place_ref[0] // 2) % 2
    coef_ref[:54, :] = of_time(link_ref, odd)
    store_left(lambda p, c: jnp.concatenate([v0_ref[p, c], v1_ref[p, c]], axis=0), left_ref)
    coef = coef_ref[...].T
    half = v0_ref.shape[2] // LZ

    def at(row, turn=False):
        if row == 2 * half:
            return row_of(halo_ref, 0)
        return row_of((v0_ref, v1_ref)[row // half], row % half, turn)

    for row in range(2 * half):
        here = coef[row * LZ : (row + 1) * LZ]
        sites = 2 * half * LZ
        store_right(right_ref.at[0], row, sites, [(here, 18, at(row + 1), False)])
        store_right(right_ref.at[1], row, sites, [(here, 36, at(row, True), False)])
    for i in range(2):
        out_ref[i] = contract(left_ref, right_ref.at[i])


def chunk(va_ref, vb_ref, vc_ref, coef, start, ahead, left_ref, right_ref):
    sites = vb_ref.shape[2]
    store_left(lambda p, c: vb_ref[p, c], left_ref)
    for row in range(sites // LZ):
        here = coef[start + row * LZ : start + (row + 1) * LZ]
        along = [(here, 56, row_of(va_ref, row), False), (here, 80, row_of(vc_ref, row), False)]
        store_right(right_ref.at[0], row, sites, along)
        store_right(right_ref.at[1], row, sites, ahead(row, here))
        store_right(right_ref.at[2], row, sites, [(here, 36, row_of(vb_ref, row, True), False)])
    return [contract(left_ref, right_ref.at[i]) for i in range(3)]


def first_kernel(place_ref, va_ref, vb_ref, vc_ref, link_a, link_b, link_c, own_ref,
                 out_ref, turned_ref, left_ref, right_ref, coef_ref):
    width = vb_ref.shape[3]
    rows = vb_ref.shape[2] // LZ
    odd = (place_ref[0] // 2) % 2
    coef_ref[:54, :] = of_time(link_b, odd)
    there = coef_ref[:18, :]
    before = adjoint_rows(of_time(link_a, odd)[:18])
    after = adjoint_rows(of_time(link_c, odd))
    coef_ref[56:74, :] = jnp.where(odd == 0, before, there)
    coef_ref[80:98, :] = jnp.where(odd == 0, there, after)
    turned_ref[...] = coef_ref[...].T
    coef = turned_ref[...]

    def ahead(row, here):
        return [(here, 18, row_of(vb_ref, row + 1), False)] if row + 1 < rows else []

    sums = chunk(va_ref, vb_ref, vc_ref, coef, 0, ahead, left_ref, right_ref)
    for i, value in enumerate(sums):
        out_ref[i * width : (i + 1) * width, :] = value + own_ref[i - 1] if i else value


def last_kernel(place_ref, va_ref, vb_ref, vc_ref, before_ref, halo_ref, turned_ref, first_ref,
                keep_ref, send_ref, left_ref, right_ref, total_ref):
    sites, width = vb_ref.shape[2], vb_ref.shape[3]
    rows = sites // LZ
    coef = turned_ref[...]

    def ahead(row, here):
        field = row_of(vb_ref, row + 1) if row + 1 < rows else row_of(halo_ref, 0)
        out = [(here, 18, field, False)]
        if row == 0:
            out.append((coef[sites - LZ : sites], 18, row_of(before_ref, rows - 1), True))
        return out

    sums = chunk(va_ref, vb_ref, vc_ref, coef, sites, ahead, left_ref, right_ref)
    for i, value in enumerate(sums):
        at = slice(i * width, (i + 1) * width)
        total_ref[at, :] = value + first_ref[at, :]
    core = place_ref[0] % 2
    half = 3 * width // 2
    keep_ref[...] = total_ref[pl.ds(pl.multiple_of(core * half, 8), half), :]
    send_ref[...] = total_ref[pl.ds(pl.multiple_of((1 - core) * half, 8), half), :]


def spread_kernel(place_ref, keep_ref, got_ref, *refs):
    outs, total_ref = refs[:-1], refs[-1]
    total_ref[...] = keep_ref[...] + got_ref[...]
    count = len(outs)
    size = outs[0].shape[0]
    pair = place_ref[0] // 4
    for d in range(count):
        at = lax.rem(pair + d, count) * size
        outs[d][...] = total_ref[pl.ds(pl.multiple_of(at, 8), size), :]


def sum_kernel(*refs):
    total = refs[0][...]
    for ref in refs[1:-1]:
        total = total + ref[...]
    refs[-1][...] = total


def table_kernel(p_ref, b_high, b_low, q_high, q_low):
    width = p_ref.shape[2] // 4
    cols = p_ref.shape[1]

    def spin(part, a):
        return p_ref[part, :, a * width : (a + 1) * width]

    m = [0.5 * (spin(0, a) - spin(1, a)) for a in (2, 3)]
    s = [0.5 * (spin(0, a) + spin(1, a)) for a in (2, 3)]
    pieces = {"m0": split(m[0]), "m1": split(m[1]), "s0": split(s[0]), "s1": split(s[1])}
    table = (
        ("+m1", "+s1", "+m0", "+s0"),
        ("+s1", "-m1", "-s0", "+m0"),
        ("+m0", "+s0", "-m1", "-s1"),
        ("-s1", "+m1", "-s0", "+m0"),
        ("+m1", "+s1", "-m0", "-s0"),
        ("-s0", "+m0", "+s1", "-m1"),
    )
    for k, names in enumerate(table):
        for j, name in enumerate(names):
            high, low = pieces[name[1:]]
            if name[0] == "-":
                high, low = -high, -low
            where = (slice(j * cols, (j + 1) * cols), slice(k * width, (k + 1) * width))
            b_high[where] = high
            b_low[where] = low
    for a in range(2):
        for part in range(2):
            high, low = split(spin(part, a))
            at = (a * 2 + part) * width
            q_high[:, at : at + width] = high
            q_low[:, at : at + width] = low


def take(ref, at, rows):
    if rows % 8 == 0:
        return ref[pl.ds(pl.multiple_of(at, 8), rows), :]
    inner = lax.rem(at, 8)
    tile = ref[pl.ds(pl.multiple_of(at - inner, 8), 8), :]
    return pltpu.roll(tile, lax.rem(8 - inner, 8), 0)[:rows]


def final_kernel(place_ref, direct_ref, slice_ref, block_ref, b_high, b_low, q_high, q_low,
                 *refs):
    count = (len(refs) - 4) // 4
    pieces = refs[: 4 * count]
    elem_ref, out_ref, all_ref, turn_ref = refs[4 * count :]
    size, width = pieces[0].shape
    place = place_ref[0]
    core = place % 2
    odd = (place // 2) % 2
    pair = place // 4
    half = 3 * width // 2
    for side in range(2):
        for other in range(2):
            for d in range(count):
                time = (odd + other) % 2
                base = (time * 2 + (core + side) % 2) * half
                at = base + lax.rem(pair - d + count, count) * size
                piece = pieces[(side * 2 + other) * count + d]
                all_ref[pl.ds(pl.multiple_of(at, 8), size), :] = piece[...]
    rows = elem_ref.shape[3]
    first = place * rows
    lane = pl.multiple_of((first // 128) * 128, 128)
    for i in range(6):
        block = all_ref[i * width : (i + 1) * width, pl.ds(lane, 128)]
        turn_ref[i * 128 : (i + 1) * 128, :] = block.T
    inner = lax.rem(first, 128)
    for g in range(2):
        time = jnp.where(slice_ref[0] == g, 0, 1)
        for k in range(3):
            which = time * 3 + direct_ref[k]
            row = take(all_ref, which * width + first, rows)
            col = take(turn_ref, which * 128 + inner, rows)
            elem_ref[g, k, 0] = 0.5 * (row - col)
            elem_ref[g, k, 1] = 0.5 * (row + col)
    time = jnp.where(slice_ref[0] == block_ref[0], 0, 1)
    turned = None
    for k in range(3):
        at = pl.multiple_of((time * 3 + direct_ref[k]) * width, 8)
        parts = split(all_ref[pl.ds(at, width), :])
        one = slice(k * width, (k + 1) * width)
        two = slice((3 + k) * width, (4 + k) * width)
        term = dot3((b_high[:, one], b_low[:, one]), parts, NT_DIMS) + dot3(
            (b_high[:, two], b_low[:, two]), parts, NN_DIMS
        )
        turned = term if turned is None else turned + term
    cols = q_high.shape[0]
    y = [turned[j * cols : (j + 1) * cols] for j in range(4)]
    same = split(jnp.concatenate([y[0], y[1], y[2], y[3]], axis=1))
    cross = split(jnp.concatenate([y[1], -y[0], y[3], -y[2]], axis=1))
    q = (q_high[...], q_low[...])
    out_ref[0] = dot3(q, cross, NT_DIMS) - dot3(cross, q, NT_DIMS)
    out_ref[1] = -(dot3(q, same, NT_DIMS) + dot3(same, q, NT_DIMS))


def shape(*dims, dtype=jnp.float32):
    return jax.ShapeDtypeStruct(dims, dtype)


def size_of(x):
    return x.size * jnp.dtype(x.dtype).itemsize


def call(kernel, out, operands, scalars=0, scratch=(), flops=0):
    outs = jax.tree.leaves(out)
    moved = sum(size_of(x) for x in list(operands) + outs)
    held = sum(int(np.prod(x.shape)) * jnp.dtype(x.dtype).itemsize for x in scratch)
    limit = moved + held + (4 << 20)
    return pl.pallas_call(
        kernel,
        out_shape=out,
        in_specs=[SMEM] * scalars + [VMEM] * (len(operands) - scalars),
        out_specs=jax.tree.map(lambda _: VMEM, out),
        scratch_shapes=list(scratch),
        cost_estimate=pl.CostEstimate(flops=flops, bytes_accessed=moved, transcendentals=0),
        compiler_params=pltpu.CompilerParams(vmem_limit_bytes=limit),
    )(*operands)


def program(vectors, links, directions, slice_group, peram, block_group):
    total = lax.axis_size("space")
    place = lax.axis_index("space")
    places = jnp.full((1,), place, jnp.int32)
    sites, width = vectors.shape[3], vectors.shape[4]
    pairs = total // 4
    odd = (place // 2) % 2

    def send(value, where):
        route = []
        for i in range(total):
            pair, o, core = where(i // 4, (i // 2) % 2, i % 2)
            route.append((i, ((pair % pairs) * 2 + o) * 2 + core))
        return lax.ppermute(value, "space", route)

    partner = lambda pair, o, core: (pair, 1 - o, core)
    twin = lambda pair, o, core: (pair, o, 1 - core)
    along = lambda pair, o, core: (pair + (1 if o else -1), o, core)

    def shift(d):
        return lambda pair, o, core: (pair + d, o, core)

    flat = links.transpose(0, 1, 3, 4, 2, 5).reshape(links.shape[0] * 54, sites)
    part = sites // 2

    def cut(time, i):
        block = (1,) + vectors.shape[1:3] + (part, width)
        return lax.dynamic_slice(vectors, (time, 0, 0, i * part, 0), block)[0]

    mine = [cut(odd, i) for i in range(2)]
    theirs = [cut(1 - odd, i) for i in range(2)]
    vec_b, vec_c = [], []
    for i in range(2):
        vec_b.append(send(theirs[i], partner))
        vec_c.append(send(mine[i], along))
    link_b = send(flat, partner)
    rows = flat.reshape(links.shape[0], 54, sites)[:, :18]
    link_c = send(rows.reshape(links.shape[0] * 18, sites), along)
    halo_a = send(mine[0][:, :, :LZ], twin)
    halo_b = send(vec_b[0][:, :, :LZ], twin)

    def left(n):
        return pltpu.VMEM((2, 2 * width, 6 * n), jnp.bfloat16)

    def right(count, n):
        return pltpu.VMEM((count, 2, 6 * n, width), jnp.bfloat16)

    coef = pltpu.VMEM((128, sites), jnp.float32)
    work = 6 * 6 * sites * 2 * width * width
    own = call(own_kernel, shape(2, width, width), (places, *mine, halo_a, flat), scalars=1,
               scratch=(left(sites), right(2, sites), coef), flops=2 * work)
    cols = peram.shape[2]
    turned = jnp.swapaxes(peram, 1, 2)
    bf16 = jnp.bfloat16
    tables = call(
        table_kernel,
        (shape(4 * cols, 6 * width, dtype=bf16),) * 2
        + (shape(cols, 4 * width, dtype=bf16),) * 2,
        (turned,))
    half = 3 * width // 2
    first, turned = call(
        first_kernel, (shape(3 * width, width), shape(sites, 128)),
        (places, mine[0], vec_b[0], vec_c[0], flat, link_b, link_c, own), scalars=1,
        scratch=(left(part), right(3, part), coef), flops=2 * work)
    keep, give = call(
        last_kernel, (shape(half, width),) * 2,
        (places, mine[1], vec_b[1], vec_c[1], vec_b[0], halo_b, turned, first), scalars=1,
        scratch=(left(part), right(3, part), pltpu.VMEM((3 * width, width), jnp.float32)),
        flops=2 * work)
    got = send(give, twin)
    size = half // pairs
    spread = call(spread_kernel, (shape(size, width),) * pairs, (places, keep, got), scalars=1,
                  scratch=(pltpu.VMEM((half, width), jnp.float32),))

    parts = [spread[0]] + [send(spread[d], shift(d)) for d in range(1, pairs)]
    shard = call(sum_kernel, shape(size, width), parts)
    here = [shard] + [send(shard, shift(d)) for d in range(1, pairs)]
    there = [send(here[0], partner)]
    for d in range(1, pairs):
        if d == 1:
            there.append(send(there[0], shift(d)))
        else:
            there.append(send(here[d], partner))
    pieces = here + there
    pieces = pieces + [send(x, twin) for x in pieces]

    return call(
        final_kernel,
        (shape(2, 3, 2, width // total, width), shape(2, cols, cols)),
        (places, directions, slice_group, block_group, *tables, *pieces), scalars=4,
        scratch=(pltpu.VMEM((6 * width, width), jnp.float32),
                 pltpu.VMEM((6 * 128, width), jnp.float32)),
        flops=36 * cols * width * width)


def solution(mesh):
    return jax.shard_map(
        program,
        mesh=mesh,
        in_specs=(
            P("cfg", None, None, "space", None),
            P("cfg", None, None, None, None, "space"),
            P(),
            P(),
            P("cfg", None, "space"),
            P("space"),
        ),
        out_specs=(P("cfg", None, None, "space", None), P("cfg", "space", None)),
        check_vma=False,
    )
```

```python
import functools

import jax
import jax.numpy as jnp
import numpy as np
from jax import lax
from jax.experimental import pallas as pl
from jax.experimental.pallas import tpu as pltpu
from jax.sharding import PartitionSpec as P

LZ = 16
VMEM = pl.BlockSpec(memory_space=pltpu.VMEM)
SMEM = pl.BlockSpec(memory_space=pltpu.SMEM)
NT_DIMS = (((1,), (1,)), ((), ()))
NN_DIMS = (((1,), (0,)), ((), ()))


def split(value):
    high = value.astype(jnp.bfloat16)
    low = (value - high.astype(jnp.float32)).astype(jnp.bfloat16)
    return high, low


def dot3(left, right, dims):
    dot = functools.partial(
        lax.dot_general, dimension_numbers=dims, preferred_element_type=jnp.float32
    )
    return dot(left[0], right[0]) + dot(left[0], right[1]) + dot(left[1], right[0])


def store_left(load, left_ref):
    for colour in range(3):
        real, imag = load(0, colour), load(1, colour)
        count, width = 2 * real.shape[0], real.shape[1]
        at = slice(colour * count, (colour + 1) * count)
        for i, pair in enumerate(((real, imag), (imag, -real))):
            for level, value in enumerate(split(jnp.concatenate(pair, axis=0).T)):
                left_ref[level, i * width : (i + 1) * width, at] = value


def add(total, term):
    return term if total is None else total + term


def store_right(right_ref, row, sites, sources):
    width = right_ref.shape[2]
    coefs = []
    for coef, base, _, turned in sources:
        wide = [jnp.broadcast_to(coef[:, base + j : base + j + 1], (LZ, 128)) for j in range(18)]
        if turned:
            order = [(b * 6 + a * 2, a, b) for a in range(3) for b in range(3)]
            wide = [w for at, _, _ in order for w in (-wide[at], wide[at + 1])]
        coefs.append(wide)
    for lanes in range(0, width, 128):
        cut = slice(lanes, lanes + 128)
        fields = []
        for _, _, field, _ in sources:
            real, imag = field(cut)
            fields.append(([r + i for r, i in zip(real, imag)], [r - i for r, i in zip(real, imag)]))
        for a in range(3):
            alpha = beta = None
            for wide, (plus, minus) in zip(coefs, fields):
                for b in range(3):
                    real, imag = wide[a * 6 + b * 2], wide[a * 6 + b * 2 + 1]
                    alpha = add(add(alpha, real * plus[b]), imag * minus[b])
                    beta = add(add(beta, imag * plus[b]), -(real * minus[b]))
            for part, value in enumerate((alpha, beta)):
                at = (a * 2 + part) * sites + row * LZ
                if value is None:
                    value = jnp.zeros((LZ, 128), jnp.float32)
                high, low = split(value)
                right_ref[0, at : at + LZ, cut] = high
                right_ref[1, at : at + LZ, cut] = low


def row_of(v_ref, row, turn=False):
    def load(cut):
        at = slice(row * LZ, (row + 1) * LZ)
        parts = [[v_ref[p, c, at, cut] for c in range(3)] for p in range(2)]
        if turn:
            parts = [[pltpu.roll(x, LZ - 1, 0) for x in part] for part in parts]
        return parts

    return load


def adjoint_rows(rows):
    out = []
    for a in range(3):
        for b in range(3):
            at = b * 6 + a * 2
            out += [-rows[at : at + 1], rows[at + 1 : at + 2]]
    return jnp.concatenate(out, axis=0)


def of_time(ref, odd):
    count = ref.shape[0] // 2
    return 0.5 * jnp.where(odd == 0, ref[:count], ref[count:])


def contract(left_ref, right_ref):
    left = (left_ref[0], left_ref[1])
    right = (right_ref[0], right_ref[1])
    both = dot3(left, right, NN_DIMS)
    width = right_ref.shape[2]
    return both[:width] - both[width:].T


def own_kernel(place_ref, v0_ref, v1_ref, halo_ref, link_ref, out_ref, left_ref, right_ref,
               coef_ref):
    odd = (place_ref[0] // 2) % 2
    coef_ref[:54, :] = of_time(link_ref, odd)
    store_left(lambda p, c: jnp.concatenate([v0_ref[p, c], v1_ref[p, c]], axis=0), left_ref)
    coef = coef_ref[...].T
    half = v0_ref.shape[2] // LZ

    def at(row, turn=False):
        if row == 2 * half:
            return row_of(halo_ref, 0)
        return row_of((v0_ref, v1_ref)[row // half], row % half, turn)

    for row in range(2 * half):
        here = coef[row * LZ : (row + 1) * LZ]
        sites = 2 * half * LZ
        store_right(right_ref.at[0], row, sites, [(here, 18, at(row + 1), False)])
        store_right(right_ref.at[1], row, sites, [(here, 36, at(row, True), False)])
    for i in range(2):
        out_ref[i] = contract(left_ref, right_ref.at[i])


def fill(right_ref, sites, sources):
    for row in range(sites // LZ):
        store_right(right_ref, row, sites, sources(row))


def crossing(va_ref, vc_ref, coef, start):
    def sources(row):
        here = coef[start + row * LZ : start + (row + 1) * LZ]
        return [(here, 56, row_of(va_ref, row), False), (here, 80, row_of(vc_ref, row), False)]

    return sources


def turning(vb_ref, coef, start):
    def sources(row):
        here = coef[start + row * LZ : start + (row + 1) * LZ]
        return [(here, 36, row_of(vb_ref, row, True), False)]

    return sources


def first_kernel(place_ref, va_ref, vb_ref, vc_ref, link_a, link_b, link_c, own_ref,
                 out_ref, turned_ref, left_ref, right_ref, coef_ref):
    width = vb_ref.shape[3]
    rows = vb_ref.shape[2] // LZ
    odd = (place_ref[0] // 2) % 2
    coef_ref[:54, :] = of_time(link_b, odd)
    there = coef_ref[:18, :]
    before = adjoint_rows(of_time(link_a, odd)[:18])
    after = adjoint_rows(of_time(link_c, odd))
    coef_ref[56:74, :] = jnp.where(odd == 0, before, there)
    coef_ref[80:98, :] = jnp.where(odd == 0, there, after)
    turned_ref[...] = coef_ref[...].T
    coef = turned_ref[...]

    sites = rows * LZ

    def ahead(row):
        here = coef[row * LZ : (row + 1) * LZ]
        return [(here, 18, row_of(vb_ref, row + 1), False)] if row + 1 < rows else []

    store_left(lambda p, c: vb_ref[p, c], left_ref)
    fill(right_ref.at[0], sites, crossing(va_ref, vc_ref, coef, 0))
    fill(right_ref.at[1], sites, ahead)
    fill(right_ref.at[2], sites, turning(vb_ref, coef, 0))
    for i in range(3):
        value = contract(left_ref, right_ref.at[i])
        out_ref[i * width : (i + 1) * width, :] = value + own_ref[i - 1] if i else value


def inner_kernel(place_ref, vb_ref, before_ref, halo_ref, turned_ref, first_ref,
                 keep_ref, send_ref, left_ref, right_ref, both_ref):
    sites, width = vb_ref.shape[2], vb_ref.shape[3]
    rows = sites // LZ
    coef = turned_ref[...]

    def ahead(row):
        here = coef[sites + row * LZ : sites + (row + 1) * LZ]
        field = row_of(vb_ref, row + 1) if row + 1 < rows else row_of(halo_ref, 0)
        out = [(here, 18, field, False)]
        if row == 0:
            out.append((coef[sites - LZ : sites], 18, row_of(before_ref, rows - 1), True))
        return out

    store_left(lambda p, c: vb_ref[p, c], left_ref)
    fill(right_ref.at[0], sites, ahead)
    fill(right_ref.at[1], sites, turning(vb_ref, coef, sites))
    for i in range(2):
        value = contract(left_ref, right_ref.at[i])
        at = slice((i + 1) * width, (i + 2) * width)
        both_ref[i * width : (i + 1) * width, :] = value + first_ref[at, :]
    core = place_ref[0] % 2
    keep_ref[...] = both_ref[pl.ds(pl.multiple_of(core * width, 8), width), :]
    send_ref[...] = both_ref[pl.ds(pl.multiple_of((1 - core) * width, 8), width), :]


def last_kernel(place_ref, va_ref, vc_ref, left_ref, turned_ref, first_ref,
                keep_ref, send_ref, right_ref, total_ref):
    sites, width = va_ref.shape[2], va_ref.shape[3]
    fill(right_ref, sites, crossing(va_ref, vc_ref, turned_ref[...], sites))
    total_ref[...] = contract(left_ref, right_ref) + first_ref[:width, :]
    core = place_ref[0] % 2
    half = width // 2
    keep_ref[...] = total_ref[pl.ds(pl.multiple_of(core * half, 8), half), :]
    send_ref[...] = total_ref[pl.ds(pl.multiple_of((1 - core) * half, 8), half), :]


def spread_kernel(place_ref, keep_ref, got_ref, keep_x_ref, got_x_ref, *refs):
    outs, total_ref = refs[:-1], refs[-1]
    width = keep_ref.shape[0]
    total_ref[:width, :] = keep_ref[...] + got_ref[...]
    total_ref[width:, :] = keep_x_ref[...] + got_x_ref[...]
    count = len(outs)
    size = outs[0].shape[0]
    pair = place_ref[0] // 4
    for d in range(count):
        at = lax.rem(pair + d, count) * size
        outs[d][...] = total_ref[pl.ds(pl.multiple_of(at, 8), size), :]


def sum_kernel(*refs):
    total = refs[0][...]
    for ref in refs[1:-1]:
        total = total + ref[...]
    refs[-1][...] = total


def table_kernel(p_ref, b_high, b_low, q_high, q_low):
    width = p_ref.shape[2] // 4
    cols = p_ref.shape[1]

    def spin(part, a):
        return p_ref[part, :, a * width : (a + 1) * width]

    m = [0.5 * (spin(0, a) - spin(1, a)) for a in (2, 3)]
    s = [0.5 * (spin(0, a) + spin(1, a)) for a in (2, 3)]
    pieces = {"m0": split(m[0]), "m1": split(m[1]), "s0": split(s[0]), "s1": split(s[1])}
    table = (
        ("+m1", "+s1", "+m0", "+s0"),
        ("+s1", "-m1", "-s0", "+m0"),
        ("+m0", "+s0", "-m1", "-s1"),
        ("-s1", "+m1", "-s0", "+m0"),
        ("+m1", "+s1", "-m0", "-s0"),
        ("-s0", "+m0", "+s1", "-m1"),
    )
    for k, names in enumerate(table):
        for j, name in enumerate(names):
            high, low = pieces[name[1:]]
            if name[0] == "-":
                high, low = -high, -low
            where = (slice(j * cols, (j + 1) * cols), slice(k * width, (k + 1) * width))
            b_high[where] = high
            b_low[where] = low
    for a in range(2):
        for part in range(2):
            high, low = split(spin(part, a))
            at = (a * 2 + part) * width
            q_high[:, at : at + width] = high
            q_low[:, at : at + width] = low


def take(ref, at, rows):
    if rows % 8 == 0:
        return ref[pl.ds(pl.multiple_of(at, 8), rows), :]
    inner = lax.rem(at, 8)
    tile = ref[pl.ds(pl.multiple_of(at - inner, 8), 8), :]
    return pltpu.roll(tile, lax.rem(8 - inner, 8), 0)[:rows]


def final_kernel(place_ref, direct_ref, slice_ref, block_ref, b_high, b_low, q_high, q_low,
                 *refs):
    count = (len(refs) - 4) // 4
    pieces = refs[: 4 * count]
    elem_ref, out_ref, all_ref, turn_ref = refs[4 * count :]
    size, width = pieces[0].shape
    place = place_ref[0]
    core = place % 2
    odd = (place // 2) % 2
    pair = place // 4
    half = 3 * width // 2
    for side in range(2):
        for other in range(2):
            for d in range(count):
                time = (odd + other) % 2
                base = (time * 2 + (core + side) % 2) * half
                at = base + lax.rem(pair - d + count, count) * size
                piece = pieces[(side * 2 + other) * count + d]
                all_ref[pl.ds(pl.multiple_of(at, 8), size), :] = piece[...]
    rows = elem_ref.shape[3]
    first = place * rows
    lane = pl.multiple_of((first // 128) * 128, 128)
    block = width // 2

    def start(time, way, h):
        inside = jnp.where(way == 0, h * half + width, (way - 1) * half + h * block)
        return time * 2 * half + inside

    for i in range(6):
        for h in range(2):
            core, at = (h, width) if i % 3 == 0 else (i % 3 - 1, h * block)
            at += (i // 3 * 2 + core) * half
            piece = all_ref[at : at + block, pl.ds(lane, 128)]
            turn_ref[i * 128 : (i + 1) * 128, h * block : (h + 1) * block] = piece.T
    inner = lax.rem(first, 128)
    for g in range(2):
        time = jnp.where(slice_ref[0] == g, 0, 1)
        for k in range(3):
            way = direct_ref[k]
            which = time * 3 + way
            row = take(all_ref, start(time, way, first // block) + lax.rem(first, block), rows)
            col = take(turn_ref, which * 128 + inner, rows)
            elem_ref[g, k, 0] = 0.5 * (row - col)
            elem_ref[g, k, 1] = 0.5 * (row + col)
    time = jnp.where(slice_ref[0] == block_ref[0], 0, 1)
    turned = None
    for k in range(3):
        places = [pl.multiple_of(start(time, direct_ref[k], h), 8) for h in range(2)]
        parts = split(jnp.concatenate([all_ref[pl.ds(at, block), :] for at in places], axis=0))
        one = slice(k * width, (k + 1) * width)
        two = slice((3 + k) * width, (4 + k) * width)
        term = dot3((b_high[:, one], b_low[:, one]), parts, NT_DIMS) + dot3(
            (b_high[:, two], b_low[:, two]), parts, NN_DIMS
        )
        turned = term if turned is None else turned + term
    cols = q_high.shape[0]
    y = [turned[j * cols : (j + 1) * cols] for j in range(4)]
    same = split(jnp.concatenate([y[0], y[1], y[2], y[3]], axis=1))
    cross = split(jnp.concatenate([y[1], -y[0], y[3], -y[2]], axis=1))
    q = (q_high[...], q_low[...])
    out_ref[0] = dot3(q, cross, NT_DIMS) - dot3(cross, q, NT_DIMS)
    out_ref[1] = -(dot3(q, same, NT_DIMS) + dot3(same, q, NT_DIMS))


def shape(*dims, dtype=jnp.float32):
    return jax.ShapeDtypeStruct(dims, dtype)


def size_of(x):
    return x.size * jnp.dtype(x.dtype).itemsize


def call(kernel, out, operands, scalars=0, scratch=(), flops=0):
    outs = jax.tree.leaves(out)
    moved = sum(size_of(x) for x in list(operands) + outs)
    held = sum(int(np.prod(x.shape)) * jnp.dtype(x.dtype).itemsize for x in scratch)
    limit = moved + held + (4 << 20)
    return pl.pallas_call(
        kernel,
        out_shape=out,
        in_specs=[SMEM] * scalars + [VMEM] * (len(operands) - scalars),
        out_specs=jax.tree.map(lambda _: VMEM, out),
        scratch_shapes=list(scratch),
        cost_estimate=pl.CostEstimate(flops=flops, bytes_accessed=moved, transcendentals=0),
        compiler_params=pltpu.CompilerParams(vmem_limit_bytes=limit),
    )(*operands)


def program(vectors, links, directions, slice_group, peram, block_group):
    total = lax.axis_size("space")
    place = lax.axis_index("space")
    places = jnp.full((1,), place, jnp.int32)
    sites, width = vectors.shape[3], vectors.shape[4]
    pairs = total // 4
    odd = (place // 2) % 2

    def send(value, where):
        route = []
        for i in range(total):
            pair, o, core = where(i // 4, (i // 2) % 2, i % 2)
            route.append((i, ((pair % pairs) * 2 + o) * 2 + core))
        return lax.ppermute(value, "space", route)

    partner = lambda pair, o, core: (pair, 1 - o, core)
    twin = lambda pair, o, core: (pair, o, 1 - core)
    along = lambda pair, o, core: (pair + (1 if o else -1), o, core)

    def shift(d):
        return lambda pair, o, core: (pair + d, o, core)

    flat = links.transpose(0, 1, 3, 4, 2, 5).reshape(links.shape[0] * 54, sites)
    part = sites // 2

    def cut(time, i):
        block = (1,) + vectors.shape[1:3] + (part, width)
        return lax.dynamic_slice(vectors, (time, 0, 0, i * part, 0), block)[0]

    mine = [cut(odd, i) for i in range(2)]
    theirs = [cut(1 - odd, i) for i in range(2)]
    vec_b, vec_c = [], []
    for i in range(2):
        vec_b.append(send(theirs[i], partner))
        vec_c.append(send(mine[i], along))
    link_b = send(flat, partner)
    rows = flat.reshape(links.shape[0], 54, sites)[:, :18]
    link_c = send(rows.reshape(links.shape[0] * 18, sites), along)
    halo_a = send(mine[0][:, :, :LZ], twin)
    halo_b = send(vec_b[0][:, :, :LZ], twin)

    def left(n):
        return pltpu.VMEM((2, 2 * width, 6 * n), jnp.bfloat16)

    def right(count, n):
        return pltpu.VMEM((count, 2, 6 * n, width), jnp.bfloat16)

    coef = pltpu.VMEM((128, sites), jnp.float32)
    work = 6 * 6 * sites * 2 * width * width
    own = call(own_kernel, shape(2, width, width), (places, *mine, halo_a, flat), scalars=1,
               scratch=(left(sites), right(2, sites), coef), flops=2 * work)
    cols = peram.shape[2]
    turned = jnp.swapaxes(peram, 1, 2)
    bf16 = jnp.bfloat16
    tables = call(
        table_kernel,
        (shape(4 * cols, 6 * width, dtype=bf16),) * 2
        + (shape(cols, 4 * width, dtype=bf16),) * 2,
        (turned,))
    half = 3 * width // 2
    first, turned = call(
        first_kernel, (shape(3 * width, width), shape(sites, 128)),
        (places, mine[0], vec_b[0], vec_c[0], flat, link_b, link_c, own), scalars=1,
        scratch=(left(part), right(3, part), coef), flops=2 * work)
    keep, give, turned_left = call(
        inner_kernel,
        (shape(width, width),) * 2 + (shape(2, 2 * width, 6 * part, dtype=bf16),),
        (places, vec_b[1], vec_b[0], halo_b, turned, first), scalars=1,
        scratch=(right(2, part), pltpu.VMEM((2 * width, width), jnp.float32)), flops=2 * work)
    got = send(give, twin)
    keep_x, give_x = call(
        last_kernel, (shape(width // 2, width),) * 2,
        (places, mine[1], vec_c[1], turned_left, turned, first), scalars=1,
        scratch=(pltpu.VMEM((2, 6 * part, width), bf16),
                 pltpu.VMEM((width, width), jnp.float32)), flops=2 * work)
    got_x = send(give_x, twin)
    size = half // pairs
    spread = call(spread_kernel, (shape(size, width),) * pairs, (places, keep, got, keep_x, got_x), scalars=1,
                  scratch=(pltpu.VMEM((half, width), jnp.float32),))

    parts = [spread[0]] + [send(spread[d], shift(d)) for d in range(1, pairs)]
    shard = call(sum_kernel, shape(size, width), parts)
    here = [shard] + [send(shard, shift(d)) for d in range(1, pairs)]
    there = [send(here[0], partner)]
    for d in range(1, pairs):
        if d == 1:
            there.append(send(there[0], shift(d)))
        else:
            there.append(send(here[d], partner))
    pieces = here + there
    pieces = pieces + [send(x, twin) for x in pieces]

    return call(
        final_kernel,
        (shape(2, 3, 2, width // total, width), shape(2, cols, cols)),
        (places, directions, slice_group, block_group, *tables, *pieces), scalars=4,
        scratch=(pltpu.VMEM((6 * width, width), jnp.float32),
                 pltpu.VMEM((6 * 128, width), jnp.float32)),
        flops=36 * cols * width * width)


def solution(mesh):
    return jax.shard_map(
        program,
        mesh=mesh,
        in_specs=(
            P("cfg", None, None, "space", None),
            P("cfg", None, None, None, None, "space"),
            P(),
            P(),
            P("cfg", None, "space"),
            P("space"),
        ),
        out_specs=(P("cfg", None, None, "space", None), P("cfg", "space", None)),
        check_vma=False,
    )
```
